256 devices in a mesh: tok: 32 (over z_hi, x, core), lyr: 8 (over z_lo, y).
Axes of the slice: x: 4, y: 4, z: 8 (z_hi: 4, z_lo: 2; z = z_hi * 2 + z_lo), core: 2. Of those that a mesh axis runs over, the one named last changes fastest.
Arguments:
- feature_codes: bfloat16 [16, 4096, 2, 256], P('lyr', 'tok'), may hold values from 0 to 21, as said below
- block_ids: int32 [16, 4096, 2], P('lyr', 'tok'), may hold values from 0 to 31, all different within a row; in each aligned block of 128 rows (0 to 127, 128 to 255, ..., all dimensions but the last counted through in order) at most 16 rows name the same one
- target_layer: int32 [4096], P('tok'), may hold values from 0 to 15
- request_ids: int32 [4096], P('tok'), may hold values from 0 to 15
- target_resid: bfloat16 [4096, 2304], P('tok'), may hold values from -6 to 6
- decoder: bfloat16 [16, 8192, 2304], P('lyr', 'tok'), may hold values from -0.25 to 0.25
Outputs:
- scores: bfloat16 [16, 4096, 2, 256], P('lyr', 'tok')
- request_totals: float32 [16, 16, 8192], P(None, 'lyr', 'tok')
The draws below stay inside these ranges and needn't reach their ends.
Inputs may be any that keep to these rules, and one draw needn't show every extreme that they name: `block_ids`: the 2 panel indices of one token at one source layer are distinct; among the 128 tokens of one index of tok at one source layer no panel is named by more than 16 of them, a bound that some block reaches. `feature_codes`: nonnegative, with many entries zero.
All inputs are finite; a program needn't handle non-finite values.
Results may differ from the reference program's by a relative error of at most 0.0053.
Values may be sent and summed in bfloat16 or wider, within the bound.
No kernel may reach another device: no remote copies, remote signals or barrier semaphores. Data moves between devices by JAX's collectives and lax.ppermute only.
A program may use at most 64 MiB of HBM per device.

```python
import math
import jax
import jax.numpy as jnp
import numpy as np
from jax import lax

D = 2304
PANEL = 256
PANELS = 32
KACT = 2
REQUESTS = 16
TOK_DEV = 128
CAP = 16
F = 8192
LAYERS = 16
TOKENS = 4096
N_TOK = 32


def draw_feature_codes(key, part):
    normal_key, scale_key = jax.random.split(jax.random.fold_in(key, 17))
    normal_part = jax.random.normal(normal_key, (LAYERS, TOKENS, KACT, PANEL), jnp.float32)
    spread = jnp.exp(jax.random.uniform(scale_key, (LAYERS, TOKENS, KACT, 1), jnp.float32, jnp.log(0.5), jnp.log(2.0)))
    return (jnp.clip(normal_part, 0.0, 5.0) * spread).astype(jnp.bfloat16)


def touch_ends(array, rng, least, high):
    dims = array.shape
    spot = [jax.random.randint(jax.random.fold_in(rng, axis), (), 0, dims[axis]) for axis in range(len(dims))]
    array = array.at[tuple(spot)].set(least)
    longest = dims.index(max(dims))
    spot[longest] = (spot[longest] + 1) % dims[longest]
    return array.at[tuple(spot)].set(high)


def block_scale(key, dims, pieces, low, largest):
    level = 1.0
    for position, parts in pieces:
        draws = jax.random.uniform(jax.random.fold_in(jax.random.fold_in(key, 6), position), (parts,), jnp.float32, low / len(pieces), largest / len(pieces))
        level = level * jnp.repeat(jnp.exp(draws), dims[position] // parts).reshape((-1,) + (1,) * (len(dims) - 1 - position))
    return level


def shared_out(stream_key, own, number, rows, count, top, bound, slope):
    sequence = jax.random.permutation(stream_key, count)
    heavy_load, usual = shares(count, rows * top, bound, slope, True), shares(count, rows * top, bound, slope, False)
    places = jnp.arange(count)

    def named(sizes, turn):
        used = int((sizes > 0).sum())
        fixed = max(1, used // 4)
        passed = fixed + (places - fixed + turn * (used - fixed)) % max(1, count - fixed)
        return jnp.zeros((count,), jnp.int32).at[sequence[jnp.where(places < fixed, places, passed)]].set(jnp.asarray(sizes, jnp.int32))

    sizes = jnp.where(number % 4 == 0, named(heavy_load, number // 4), named(usual, number - number // 4 - 1))
    mixed = jax.random.permutation(jax.random.fold_in(own, 3), count)
    giver, sink = mixed[0:count // 2 * 2:2], mixed[1:count // 2 * 2:2]
    margin = jnp.minimum(sizes[giver] - 1, bound - sizes[sink]) // 2
    margin = jnp.where((giver == sequence[0]) | (sink == sequence[0]) | (sizes[sink] == 0), 0, jnp.maximum(margin, 0))
    passed = jax.random.randint(jax.random.fold_in(own, 4), (count // 2,), 0, 1 << 20) % (margin + 1)
    sizes = sizes.at[giver].add(-passed).at[sink].add(passed)
    items = jnp.searchsorted(jnp.cumsum(sizes), jnp.arange(rows * top), side="right").astype(jnp.int32)
    table = items.reshape(top, rows).T
    table = table[jax.random.permutation(jax.random.fold_in(own, 1), rows)]
    turn = jax.random.randint(jax.random.fold_in(own, 2), (rows, 1), 0, top)
    return jnp.take_along_axis(table, (jnp.arange(top)[None, :] + turn) % top, axis=1)


def shares(amount, total, limit, skew, full):
    loads = [(1 << 20) // math.isqrt(rank ** skew) + 1 for rank in range(1, amount + 1)]
    largest = limit if full else min(limit, max(-(-total // amount), total * loads[0] // sum(loads)))
    least = 1 if total - largest >= amount - 1 else 0
    holding, rest = [largest] + [least] * (amount - 1), total - largest - least * (amount - 1)
    while rest > 0:
        free = [i for i in range(1, amount) if holding[i] < largest] or [i for i in range(1, amount) if holding[i] < limit]
        whole, remaining = sum([loads[i] for i in free]), rest
        for i in free:
            extra = min(limit - holding[i], max(1, remaining * loads[i] // whole), rest)
            holding[i] = holding[i] + extra
            rest = rest - extra
    return np.array(holding)


def bell_draw(stream_key, dims, scale, most, pieces=(), held_as=jnp.bfloat16):
    drawn = jax.random.normal(stream_key, dims, jnp.float32) * scale
    if len(pieces) > 0:
        drawn = block_scale(stream_key, dims, pieces, -0.22, 0.18) * drawn
    return jnp.clip(drawn, min=-most, max=most).astype(held_as)


def setup_inputs(seed: int = 0) -> dict:
    arg_keys = jax.random.split(jax.random.key(seed), 7)
    feature_codes = draw_feature_codes(jax.random.fold_in(arg_keys[6], 71), 0)
    block_ids_keys = jax.random.split(jax.random.fold_in(arg_keys[1], 1), LAYERS * TOKENS // TOK_DEV)
    block_ids_turns = jax.random.permutation(jax.random.fold_in(arg_keys[1], 3), LAYERS * TOKENS // TOK_DEV)
    block_ids = jax.vmap(lambda own, number: shared_out(jax.random.fold_in(arg_keys[1], 2), own, number, TOK_DEV, PANELS, KACT, CAP, 1))(block_ids_keys, block_ids_turns).reshape((LAYERS, TOKENS, KACT))
    target_layer = touch_ends(jax.random.randint(arg_keys[2], (TOKENS,), 0, LAYERS), jax.random.fold_in(arg_keys[2], 1), 0, LAYERS - 1).astype(jnp.int32)
    request_ids = touch_ends(jax.random.randint(arg_keys[3], (TOKENS,), 0, REQUESTS), jax.random.fold_in(arg_keys[3], 1), 0, REQUESTS - 1).astype(jnp.int32)
    target_resid = bell_draw(arg_keys[4], (TOKENS, D), 1.0, 6.0, ((0, 32),))
    decoder = bell_draw(arg_keys[5], (LAYERS, F, D), (KACT * PANEL) ** -0.5, 0.25, ((0, 8), (1, 32)))
    return dict(feature_codes=feature_codes, block_ids=block_ids, target_layer=target_layer, request_ids=request_ids, target_resid=target_resid, decoder=decoder)


def grouped(sorted_rows, weights, counts, starts, width):
    window_size = N_TOK * CAP
    total_rows = sorted_rows.shape[0]
    positions = jnp.arange(window_size, dtype=jnp.int32)

    def add_panel(buffer, panel_index):
        offset = starts[panel_index]
        window = lax.dynamic_slice_in_dim(sorted_rows, offset, window_size, 0)
        product = jnp.dot(window, weights[panel_index], preferred_element_type=jnp.float32)
        rounded = lax.optimization_barrier(product.astype(jnp.bfloat16)).astype(jnp.float32)
        keeping = positions < counts[panel_index]
        rounded = jnp.where(keeping[:, None], rounded, jnp.zeros_like(rounded))
        current = lax.dynamic_slice_in_dim(buffer, offset, window_size, 0)
        buffer = lax.dynamic_update_slice_in_dim(buffer, current + rounded, offset, 0)
        return (buffer, None)
    initial = jnp.zeros((total_rows, width), jnp.float32)
    buffer, _ = lax.scan(add_panel, initial, jnp.arange(PANELS, dtype=jnp.int32))
    return buffer[:total_rows - window_size]

def reference(feature_codes, block_ids, target_layer, request_ids, target_resid, decoder):
    count = target_resid.shape[0]
    row_total = count * KACT
    window_size = N_TOK * CAP
    panel_iota = jnp.arange(PANELS, dtype=jnp.int32)
    row_iota = jnp.arange(row_total, dtype=jnp.int32)
    rebuilt = jnp.zeros((count, D), jnp.float32)
    saved = []
    for source in range(LAYERS):
        alive_mask = (target_layer >= source).astype(feature_codes.dtype)
        masked = feature_codes[source] * alive_mask[:, None, None]
        flat_ids = block_ids[source].reshape(row_total).astype(jnp.int32)
        ranking = jnp.argsort(flat_ids, stable=True).astype(jnp.int32)
        inverse = jnp.zeros((row_total,), jnp.int32).at[ranking].set(row_iota)
        counts = lax.optimization_barrier(jnp.sum((flat_ids[:, None] == panel_iota[None, :]).astype(jnp.int32), axis=0)).astype(jnp.int32)
        starts = (jnp.cumsum(counts) - counts).astype(jnp.int32)
        code_rows = masked.reshape(row_total, PANEL)[ranking]
        code_rows = jnp.concatenate([code_rows, jnp.zeros((window_size, PANEL), code_rows.dtype)], axis=0)
        panels = decoder[source].reshape(PANELS, PANEL, D)
        contrib = grouped(code_rows, panels, counts, starts, D)[inverse]
        rebuilt = rebuilt + lax.optimization_barrier(jnp.sum(contrib.reshape(count, KACT, D), axis=1))
        saved.append((masked, ranking, inverse, counts, starts))
    error = target_resid.astype(jnp.float32) - rebuilt
    spread = lax.optimization_barrier(jnp.mean(error * error, axis=-1, keepdims=True))
    gradient = (error * lax.rsqrt(spread + 1e-06)).astype(jnp.bfloat16)
    members = (request_ids[:, None] == jnp.arange(REQUESTS, dtype=jnp.int32)[None, :]).astype(jnp.float32)
    scores = []
    totals = []
    for source in range(LAYERS):
        masked, ranking, inverse, counts, starts = saved[source]
        token_of = ranking // KACT
        grad_rows = jnp.concatenate([gradient[token_of], jnp.zeros((window_size, D), gradient.dtype)], axis=0)
        panels_t = jnp.swapaxes(decoder[source].reshape(PANELS, PANEL, D), 1, 2)
        projected = grouped(grad_rows, panels_t, counts, starts, PANEL)[inverse].reshape(count, KACT, PANEL)
        attribution = masked.astype(jnp.float32) * projected
        scores.append(attribution.astype(jnp.bfloat16))
        summed = jnp.zeros((REQUESTS * PANELS, PANEL), jnp.float32)
        for which in range(KACT):
            panel_hot = (block_ids[source][:, which][:, None] == panel_iota[None, :]).astype(jnp.float32)
            combined = (members[:, :, None] * panel_hot[:, None, :]).reshape(count, REQUESTS * PANELS)
            summed = summed + jnp.dot(combined.T, attribution[:, which], precision=lax.Precision.HIGHEST)
        totals.append(summed.reshape(REQUESTS, PANELS * PANEL))
    return (jnp.stack(scores, axis=0), jnp.stack(totals, axis=1))
```

```python
import jax
import jax.numpy as jnp
from jax import lax
from jax.experimental import pallas as pl
from jax.experimental.pallas import tpu as pltpu
from jax.sharding import Mesh, PartitionSpec as P

PANELS = 32
REQUESTS = 16
CAP = 16
LANES = 128
TOK = ("zh", "x", "c")
LYR = ("zl", "y")
PLANE = ("y", "x", "c")
COLUMN = ("zh", "zl")
EVERY = ("zh", "x", "c", "zl", "y")
BF16 = jnp.bfloat16
F32 = jnp.float32


def call(kernel, out_shape, flops, moved, scratch=(), limit=48):
    return pl.pallas_call(
        kernel,
        out_shape=out_shape,
        scratch_shapes=list(scratch),
        compiler_params=pltpu.CompilerParams(vmem_limit_bytes=limit * 1024 * 1024),
        cost_estimate=pl.CostEstimate(flops=flops, bytes_accessed=moved, transcendentals=0),
    )


def iota(shape, axis):
    return lax.broadcasted_iota(jnp.int32, shape, axis)


def to_column(row):
    n = row.shape[1]
    diag = iota((n, n), 0) == iota((n, n), 1)
    return jnp.sum(jnp.where(diag, jnp.broadcast_to(row, (n, n)), jnp.zeros((n, n), row.dtype)), axis=1, keepdims=True)


def pack_kernel(layer_ref, ids_ref, target_ref, request_ref, codes_ref, out_ref, slot_ref):
    layers, rows = ids_ref.shape
    tokens = target_ref.shape[1]
    request = request_ref[...].astype(F32)
    request_col = to_column(jnp.concatenate([request, request], axis=1))
    token_col = (iota((rows, 1), 0) % tokens + 1).astype(F32)
    lane = iota((rows, LANES), 1)
    extra = jnp.where(lane == 0, token_col, jnp.where(lane == 1, request_col, 0.0)).astype(BF16)
    target = target_ref[...]
    target_row = jnp.concatenate([target, target], axis=1)
    for l in range(layers):
        ids_row = ids_ref[l : l + 1, :].astype(F32)
        ids_col = to_column(ids_row)
        earlier = (ids_col == ids_row) & (iota((rows, rows), 0) < iota((rows, rows), 1))
        rank = jnp.sum(jnp.where(earlier, 1.0, 0.0), axis=0, keepdims=True)
        slot = (ids_row * CAP + rank).astype(jnp.int32)
        slot = jnp.where(target_row >= layer_ref[0] + l, slot, -1)
        slot_ref[l : l + 1, :] = slot
        pick = jnp.where(iota((PANELS * CAP, rows), 0) == slot, 1.0, 0.0).astype(BF16)
        panel = codes_ref.shape[2]
        sent = jnp.dot(pick, codes_ref[l], preferred_element_type=F32).astype(BF16)
        out_ref[:, l * CAP : (l + 1) * CAP, 0:panel] = sent.reshape(PANELS, CAP, panel)
        info = jnp.dot(pick, extra, preferred_element_type=F32).astype(BF16)
        out_ref[:, l * CAP : (l + 1) * CAP, panel : panel + LANES] = info.reshape(PANELS, CAP, LANES)


def build_kernel(codes_ref, weight_ref, out_ref):
    blocks, slots, _ = codes_ref.shape
    layers, panel, width = weight_ref.shape
    step = 256

    def body(n, carry):
        cols = pl.ds(pl.multiple_of(n * step, step), step)
        for l in range(layers):
            codes = codes_ref[:, l * CAP : (l + 1) * CAP, 0:panel].reshape(blocks * CAP, panel)
            built = jnp.dot(codes, weight_ref[l, :, cols], preferred_element_type=F32).astype(BF16)
            out_ref[:, l * CAP : (l + 1) * CAP, cols] = built.reshape(blocks, CAP, step)
        return carry

    lax.fori_loop(0, width // step, body, 0)
    out_ref[:, :, width : width + LANES] = codes_ref[:, :, panel : panel + LANES]


def reduce_kernel(rows_ref, out_ref, hot_ref):
    groups, slots, wide = rows_ref.shape
    width = wide - LANES
    tokens = hot_ref.shape[1]
    count = groups * slots
    step = 256
    token = rows_ref[:, :, width : width + LANES].reshape(count, LANES).astype(F32)[:, 0:1]
    hot = jnp.where(token == (iota((count, tokens), 1) + 1).astype(F32), 1.0, 0.0)
    hot_ref[...] = hot.astype(BF16)
    hot_t = hot.T.astype(BF16)

    def body(n, carry):
        cols = pl.ds(pl.multiple_of(n * step, step), step)
        rows = rows_ref[:, :, cols].reshape(count, step)
        out_ref[:, cols] = jnp.dot(hot_t, rows, preferred_element_type=F32).astype(out_ref.dtype)
        return carry

    lax.fori_loop(0, width // step, body, 0)


def gradient_kernel(parts_ref, resid_ref, out_ref):
    planes, tokens, width = parts_ref.shape
    rebuilt = parts_ref[0].astype(F32)
    for i in range(1, planes):
        rebuilt = rebuilt + parts_ref[i].astype(F32)
    error = resid_ref[...].astype(F32) - rebuilt
    spread = jnp.sum(error * error, axis=-1, keepdims=True) * (1.0 / width)
    gradient = (error * lax.rsqrt(spread + 1e-06)).astype(BF16)
    for i in range(planes):
        out_ref[i] = gradient


def spread_kernel(hot_ref, gradient_ref, out_ref):
    groups, slots, width = out_ref.shape
    step = 256

    def body(n, carry):
        cols = pl.ds(pl.multiple_of(n * step, step), step)
        rows = jnp.dot(hot_ref[...], gradient_ref[:, cols], preferred_element_type=F32).astype(BF16)
        out_ref[:, :, cols] = rows.reshape(groups, slots, step)
        return carry

    lax.fori_loop(0, width // step, body, 0)


def project_kernel(rows_ref, codes_ref, weight_ref, score_ref, total_ref):
    blocks, slots, width = rows_ref.shape
    layers, panel, _ = weight_ref.shape
    part = 8
    total_ref[...] = jnp.zeros_like(total_ref)

    def body(m, carry):
        here = pl.ds(m * part, part)
        for l in range(layers):
            inside = slice(l * CAP, (l + 1) * CAP)
            rows = rows_ref[here, inside, :].reshape(part * CAP, width)
            projected = lax.dot_general(
                rows, weight_ref[l], (((1,), (1,)), ((), ())), preferred_element_type=F32
            ).astype(BF16)
            codes = codes_ref[here, inside, 0:panel].reshape(part * CAP, panel).astype(F32)
            request = codes_ref[here, inside, panel : panel + LANES].reshape(part * CAP, LANES).astype(F32)[:, 1:2]
            value = codes * projected.astype(F32)
            score_ref[here, inside, :] = value.astype(BF16).reshape(part, CAP, panel)
            member = jnp.where(request == iota((part * CAP, LANES), 1).astype(F32), 1.0, 0.0)
            summed = jnp.dot(member.T, value, precision=lax.Precision.HIGHEST, preferred_element_type=F32)
            total_ref[l] = total_ref[l] + summed[0:REQUESTS]
        return carry

    lax.fori_loop(0, blocks // part, body, 0)


def place_kernel(slot_ref, scores_ref, out_ref):
    layers, rows = slot_ref.shape
    panel = scores_ref.shape[2]
    for l in range(layers):
        pick_t = jnp.where(iota((PANELS * CAP, rows), 0) == slot_ref[l : l + 1, :], 1.0, 0.0)
        pick = pick_t.T.astype(BF16)
        scores = scores_ref[:, l * CAP : (l + 1) * CAP, :].reshape(PANELS * CAP, panel)
        out_ref[l] = jnp.dot(pick, scores, preferred_element_type=F32).astype(BF16)


def per_device(feature_codes, block_ids, target_layer, request_ids, target_resid, decoder):
    layers, count, kact, panel = feature_codes.shape
    width = target_resid.shape[1]
    rows = count * kact
    blocks = lax.axis_size(TOK)
    planes = lax.axis_size(COLUMN)
    share = count // planes
    slots = layers * CAP
    zh, zl, y = lax.axis_index("zh"), lax.axis_index("zl"), lax.axis_index("y")
    first_layer = lax.axis_index(LYR) * layers

    sizes = [lax.axis_size(a) for a in EVERY]
    swap = []
    for d in range(sizes[0] * sizes[1] * sizes[2] * sizes[3] * sizes[4]):
        rest, d_y = divmod(d, sizes[4])
        rest, d_zl = divmod(rest, sizes[3])
        d_zh, d_xc = divmod(rest, sizes[1] * sizes[2])
        swap.append((d, ((d_y * sizes[1] * sizes[2] + d_xc) * sizes[3] + d_zl) * sizes[4] + d_zh))
    mine = lax.dynamic_slice_in_dim(target_resid, (y * sizes[3] + zl) * share, share, 0)
    resid = lax.ppermute(mine, EVERY, swap)

    ids = block_ids.transpose(0, 2, 1).reshape(layers, rows)
    codes = feature_codes.transpose(0, 2, 1, 3).reshape(layers, rows, panel)
    layer_arr = first_layer.reshape(1).astype(jnp.int32)
    sent, slot = pl.pallas_call(
        pack_kernel,
        out_shape=(
            jax.ShapeDtypeStruct((blocks, slots, panel + LANES), BF16),
            jax.ShapeDtypeStruct((layers, rows), jnp.int32),
        ),
        in_specs=[pl.BlockSpec(memory_space=pltpu.SMEM)] + [pl.BlockSpec(memory_space=pltpu.VMEM)] * 4,
        compiler_params=pltpu.CompilerParams(vmem_limit_bytes=32 * 1024 * 1024),
        cost_estimate=pl.CostEstimate(flops=300_000_000, bytes_accessed=1_000_000, transcendentals=0),
    )(layer_arr, ids, target_layer.reshape(1, count), request_ids.reshape(1, count), codes)
    codes_in = lax.all_to_all(sent, TOK, 0, 0, tiled=True)

    built = call(
        build_kernel, jax.ShapeDtypeStruct((blocks, slots, width + LANES), BF16), 1_200_000_000, 8_000_000
    )(codes_in, decoder)
    rows_in = lax.all_to_all(built, PLANE, 0, 0, tiled=True)
    partial, hot = call(
        reduce_kernel,
        (jax.ShapeDtypeStruct((count, width), BF16), jax.ShapeDtypeStruct((blocks * slots, count), BF16)),
        600_000_000,
        6_000_000,
    )(rows_in)
    parts = lax.all_to_all(partial.reshape(planes, share, width), COLUMN, 0, 0, tiled=True)
    copies = call(gradient_kernel, jax.ShapeDtypeStruct((planes, share, width), BF16), 1_000_000, 1_200_000)(
        parts, resid
    )
    gradient = lax.all_to_all(copies, COLUMN, 0, 0, tiled=True).reshape(count, width)
    spread = call(spread_kernel, jax.ShapeDtypeStruct((blocks, slots, width), BF16), 600_000_000, 6_000_000)(
        hot, gradient
    )
    grad_in = lax.all_to_all(spread, PLANE, 0, 0, tiled=True)
    scored, totals = call(
        project_kernel,
        (
            jax.ShapeDtypeStruct((blocks, slots, panel), BF16),
            jax.ShapeDtypeStruct((layers, REQUESTS, panel), F32),
        ),
        1_300_000_000,
        8_000_000,
    )(grad_in, codes_in, decoder)
    scores_in = lax.all_to_all(scored, TOK, 0, 0, tiled=True)
    placed = call(place_kernel, jax.ShapeDtypeStruct((layers, rows, panel), BF16), 140_000_000, 1_000_000)(
        slot, scores_in
    )
    scores = placed.reshape(layers, kact, count, panel).transpose(0, 2, 1, 3)
    return scores, totals.transpose(1, 0, 2)


def solution(mesh):
    fine = Mesh(mesh.devices.reshape(4, 4, 2, 2, 4), EVERY)
    placed = (
        P(LYR, TOK, None, None),
        P(LYR, TOK, None),
        P(TOK),
        P(TOK),
        P(TOK, None),
        P(LYR, TOK, None),
    )
    return jax.shard_map(
        per_device,
        mesh=fine,
        in_specs=placed,
        out_specs=(P(LYR, TOK, None, None), P(None, LYR, TOK)),
        check_vma=False,
    )
```

```python
import jax
import jax.numpy as jnp
from jax import lax
from jax.experimental import pallas as pl
from jax.experimental.pallas import tpu as pltpu
from jax.sharding import Mesh, PartitionSpec as P

PANELS = 32
REQUESTS = 16
CAP = 16
LANES = 128
TOK = ("zh", "x", "c")
LYR = ("zl", "y")
PLANE = ("y", "x", "c")
COLUMN = ("zh", "zl")
EVERY = ("zh", "x", "c", "zl", "y")
BF16 = jnp.bfloat16
F32 = jnp.float32


def call(kernel, out_shape, flops, moved, scratch=(), limit=20):
    return pl.pallas_call(
        kernel,
        out_shape=out_shape,
        scratch_shapes=list(scratch),
        compiler_params=pltpu.CompilerParams(vmem_limit_bytes=limit * 1024 * 1024),
        cost_estimate=pl.CostEstimate(flops=flops, bytes_accessed=moved, transcendentals=0),
    )


def iota(shape, axis):
    return lax.broadcasted_iota(jnp.int32, shape, axis)


def to_column(row):
    n = row.shape[1]
    diag = iota((n, n), 0) == iota((n, n), 1)
    return jnp.sum(jnp.where(diag, jnp.broadcast_to(row, (n, n)), jnp.zeros((n, n), row.dtype)), axis=1, keepdims=True)


def lane_groups(info):
    groups = info.shape[0]
    return jnp.sum(info.reshape(groups // 4, 4, 1, LANES), axis=1)


def pack_kernel(where_ref, ids_ref, target_ref, request_ref, codes_ref, out_ref, slot_ref):
    layers, rows = ids_ref.shape
    tokens = target_ref.shape[1]
    panel = codes_ref.shape[2]
    slots = layers * CAP
    per = LANES // slots
    halves = panel // LANES
    target = target_ref[...]
    target_row = jnp.concatenate([target, target], axis=1)
    request = request_ref[...].astype(F32) + 1.0
    request_row = jnp.concatenate([request, request], axis=1)
    token_row = (iota((1, rows), 1) % tokens + 1).astype(F32)
    token_info = jnp.zeros((PANELS, LANES), F32)
    request_info = jnp.zeros((PANELS, LANES), F32)
    for l in range(layers):
        ids_row = ids_ref[l : l + 1, :].astype(F32)
        ids_col = to_column(ids_row)
        earlier = (ids_col == ids_row) & (iota((rows, rows), 0) < iota((rows, rows), 1))
        rank = jnp.sum(jnp.where(earlier, 1.0, 0.0), axis=0, keepdims=True)
        alive = target_row >= where_ref[0] + l
        slot = jnp.where(alive, (ids_row * CAP + rank).astype(jnp.int32), -1)
        slot_ref[l : l + 1, :] = slot
        pick = jnp.where(iota((PANELS * CAP, rows), 0) == slot, 1.0, 0.0).astype(BF16)
        sent = jnp.dot(pick, codes_ref[l], preferred_element_type=F32).astype(BF16)
        for h in range(halves):
            half = sent[:, h * LANES : (h + 1) * LANES]
            out_ref[:, h * slots + l * CAP : h * slots + (l + 1) * CAP, :] = half.reshape(PANELS, CAP, LANES)
        named = (iota((PANELS, rows), 0).astype(F32) == ids_row) & alive
        place = jnp.where(iota((rows, LANES), 1) % slots == to_column(rank).astype(jnp.int32) + l * CAP, 1.0, 0.0)
        place = place.astype(BF16)
        token_info += jnp.dot(jnp.where(named, token_row, 0.0).astype(BF16), place, preferred_element_type=F32)
        request_info += jnp.dot(jnp.where(named, request_row, 0.0).astype(BF16), place, preferred_element_type=F32)
    spot = iota((PANELS, LANES), 1) // slots
    token_info = jnp.where(spot == iota((PANELS, LANES), 0) % per, token_info, 0.0)
    request_info = jnp.where(spot == where_ref[1] % per, request_info, 0.0)
    line = iota((PANELS, 8, LANES), 1)
    tile = jnp.where(
        line == 0,
        token_info.reshape(PANELS, 1, LANES),
        jnp.where(line == 1, request_info.reshape(PANELS, 1, LANES), 0.0),
    )
    out_ref[:, halves * slots : halves * slots + 8, :] = tile.astype(BF16)


def build_kernel(codes_ref, weight_ref, out_ref):
    blocks = codes_ref.shape[0]
    layers, panel, width = weight_ref.shape
    slots = layers * CAP
    halves = panel // LANES
    tiles = 2

    def body(n, carry):
        cols = pl.ds(pl.multiple_of(n * tiles * LANES, LANES), tiles * LANES)
        for l in range(layers):
            codes = jnp.concatenate(
                [
                    codes_ref[:, h * slots + l * CAP : h * slots + (l + 1) * CAP, :].reshape(blocks * CAP, LANES)
                    for h in range(halves)
                ],
                axis=1,
            )
            built = jnp.dot(codes, weight_ref[l, :, cols], preferred_element_type=F32).astype(BF16)
            for i in range(tiles):
                at = pl.ds(pl.multiple_of((n * tiles + i) * slots + l * CAP, CAP), CAP)
                out_ref[:, at, :] = built[:, i * LANES : (i + 1) * LANES].reshape(blocks, CAP, LANES)
        return carry

    lax.fori_loop(0, width // (tiles * LANES), body, 0)
    end = width // LANES * slots
    out_ref[:, end : end + 8, :] = codes_ref[:, halves * slots : halves * slots + 8, :]


def reduce_kernel(rows_ref, out_ref, hot_ref):
    groups = rows_ref.shape[0]
    tokens, width = out_ref.shape
    count = hot_ref.shape[0]
    slots = count // groups
    tiles = 2
    end = width // LANES * slots
    token = lane_groups(rows_ref[:, end : end + 8, :].astype(F32)[:, 0:1, :])
    want = (iota((tokens, LANES), 0) + 1).astype(F32)
    hot_t = jnp.concatenate([jnp.where(token[g] == want, 1.0, 0.0) for g in range(count // LANES)], axis=1)
    hot_ref[...] = hot_t.T.astype(BF16)
    hot_t = hot_t.astype(BF16)

    def body(n, carry):
        rows = jnp.concatenate(
            [
                rows_ref[:, pl.ds(pl.multiple_of((n * tiles + i) * slots, slots), slots), :].reshape(count, LANES)
                for i in range(tiles)
            ],
            axis=1,
        )
        cols = pl.ds(pl.multiple_of(n * tiles * LANES, LANES), tiles * LANES)
        out_ref[:, cols] = jnp.dot(hot_t, rows, preferred_element_type=F32).astype(out_ref.dtype)
        return carry

    lax.fori_loop(0, width // (tiles * LANES), body, 0)


def gradient_kernel(parts_ref, resid_ref, out_ref):
    planes, tokens, width = parts_ref.shape
    rebuilt = parts_ref[0].astype(F32)
    for i in range(1, planes):
        rebuilt = rebuilt + parts_ref[i].astype(F32)
    error = resid_ref[...].astype(F32) - rebuilt
    spread = jnp.sum(error * error, axis=-1, keepdims=True) * (1.0 / width)
    gradient = (error * lax.rsqrt(spread + 1e-06)).astype(BF16)
    for i in range(planes):
        out_ref[i] = gradient


def spread_kernel(hot_ref, gradient_ref, out_ref):
    groups = out_ref.shape[0]
    count = hot_ref.shape[0]
    width = gradient_ref.shape[1]
    slots = count // groups
    tiles = 2

    def body(n, carry):
        cols = pl.ds(pl.multiple_of(n * tiles * LANES, LANES), tiles * LANES)
        rows = jnp.dot(hot_ref[...], gradient_ref[:, cols], preferred_element_type=F32).astype(BF16)
        for i in range(tiles):
            at = pl.ds(pl.multiple_of((n * tiles + i) * slots, slots), slots)
            out_ref[:, at, :] = rows[:, i * LANES : (i + 1) * LANES].reshape(groups, slots, LANES)
        return carry

    lax.fori_loop(0, width // (tiles * LANES), body, 0)


def project_kernel(rows_ref, codes_ref, weight_ref, score_ref, total_ref, sum_ref):
    blocks = rows_ref.shape[0]
    layers, panel, width = weight_ref.shape
    slots = layers * CAP
    halves = panel // LANES
    tiles = 2
    sum_ref[...] = jnp.zeros_like(sum_ref)

    def body(n, carry):
        cols = pl.ds(pl.multiple_of(n * tiles * LANES, LANES), tiles * LANES)
        for l in range(layers):
            rows = jnp.concatenate(
                [
                    rows_ref[:, pl.ds(pl.multiple_of((n * tiles + i) * slots + l * CAP, CAP), CAP), :].reshape(
                        blocks * CAP, LANES
                    )
                    for i in range(tiles)
                ],
                axis=1,
            )
            sum_ref[l] += lax.dot_general(
                rows, weight_ref[l, :, cols], (((1,), (1,)), ((), ())), preferred_element_type=F32
            )
        return carry

    lax.fori_loop(0, width // (tiles * LANES), body, 0)
    request = lane_groups(codes_ref[:, halves * slots : halves * slots + 8, :].astype(F32)[:, 1:2, :])
    lane_layer = iota((layers * REQUESTS, LANES), 1) % slots // CAP
    line = iota((layers * REQUESTS, LANES), 0)
    want = (line % REQUESTS + 1).astype(F32)
    here = lane_layer == line // REQUESTS
    member = jnp.concatenate(
        [jnp.where((request[g] == want) & here, 1.0, 0.0) for g in range(blocks * slots // LANES)], axis=1
    ).astype(BF16)
    for h in range(halves):
        values = []
        for l in range(layers):
            at = slice(h * slots + l * CAP, h * slots + (l + 1) * CAP)
            codes = codes_ref[:, at, :].reshape(blocks * CAP, LANES).astype(F32)
            projected = sum_ref[l, :, h * LANES : (h + 1) * LANES].astype(BF16).astype(F32)
            value = codes * projected
            score_ref[:, at, :] = value.astype(BF16).reshape(blocks, CAP, LANES)
            values.append(value.reshape(blocks, CAP, LANES))
        value = jnp.concatenate(values, axis=1).reshape(blocks * slots, LANES)
        upper = value.astype(BF16)
        lower = (value - upper.astype(F32)).astype(BF16)
        summed = jnp.dot(member, upper, preferred_element_type=F32) + jnp.dot(
            member, lower, preferred_element_type=F32
        )
        for l in range(layers):
            total_ref[l, :, h * LANES : (h + 1) * LANES] = summed[l * REQUESTS : (l + 1) * REQUESTS]


def place_kernel(slot_ref, scores_ref, out_ref):
    layers, rows = slot_ref.shape
    slots = layers * CAP
    halves = out_ref.shape[2] // LANES
    for l in range(layers):
        column = to_column(slot_ref[l : l + 1, :])
        pick = jnp.where(iota((rows, PANELS * CAP), 1) == column, 1.0, 0.0).astype(BF16)
        scores = jnp.concatenate(
            [
                scores_ref[:, h * slots + l * CAP : h * slots + (l + 1) * CAP, :].reshape(PANELS * CAP, LANES)
                for h in range(halves)
            ],
            axis=1,
        )
        out_ref[l] = jnp.dot(pick, scores, preferred_element_type=F32).astype(BF16)


def per_device(feature_codes, block_ids, target_layer, request_ids, target_resid, decoder):
    layers, count, kact, panel = feature_codes.shape
    width = target_resid.shape[1]
    rows = count * kact
    blocks = lax.axis_size(TOK)
    planes = lax.axis_size(COLUMN)
    share = count // planes
    slots = layers * CAP
    code_lines = panel // LANES * slots
    row_lines = width // LANES * slots
    zh, zl, y = lax.axis_index("zh"), lax.axis_index("zl"), lax.axis_index("y")
    first_layer = lax.axis_index(LYR) * layers

    sizes = [lax.axis_size(a) for a in EVERY]
    swap = []
    for d in range(sizes[0] * sizes[1] * sizes[2] * sizes[3] * sizes[4]):
        rest, d_y = divmod(d, sizes[4])
        rest, d_zl = divmod(rest, sizes[3])
        d_zh, d_xc = divmod(rest, sizes[1] * sizes[2])
        swap.append((d, ((d_y * sizes[1] * sizes[2] + d_xc) * sizes[3] + d_zl) * sizes[4] + d_zh))
    mine = lax.dynamic_slice_in_dim(target_resid, (y * sizes[3] + zl) * share, share, 0)
    resid = lax.ppermute(mine, EVERY, swap)

    ids = block_ids.transpose(0, 2, 1).reshape(layers, rows)
    codes = feature_codes.transpose(0, 2, 1, 3).reshape(layers, rows, panel)
    where = jnp.stack([first_layer, lax.axis_index(TOK)]).astype(jnp.int32)
    sent, slot = pl.pallas_call(
        pack_kernel,
        out_shape=(
            jax.ShapeDtypeStruct((blocks, code_lines + 8, LANES), BF16),
            jax.ShapeDtypeStruct((layers, rows), jnp.int32),
        ),
        in_specs=[pl.BlockSpec(memory_space=pltpu.SMEM)] + [pl.BlockSpec(memory_space=pltpu.VMEM)] * 4,
        compiler_params=pltpu.CompilerParams(vmem_limit_bytes=12 * 1024 * 1024),
        cost_estimate=pl.CostEstimate(flops=300_000_000, bytes_accessed=1_000_000, transcendentals=0),
    )(where, ids, target_layer.reshape(1, count), request_ids.reshape(1, count), codes)
    codes_in = lax.all_to_all(sent, TOK, 0, 0, tiled=True)

    built = call(
        build_kernel, jax.ShapeDtypeStruct((blocks, row_lines + 8, LANES), BF16), 1_200_000_000, 8_000_000
    )(codes_in, decoder)
    rows_in = lax.all_to_all(built, PLANE, 0, 0, tiled=True)
    partial, hot = call(
        reduce_kernel,
        (jax.ShapeDtypeStruct((count, width), BF16), jax.ShapeDtypeStruct((blocks * slots, count), BF16)),
        600_000_000,
        6_000_000,
    )(rows_in)
    parts = lax.all_to_all(partial.reshape(planes, share, width), COLUMN, 0, 0, tiled=True)
    copies = call(gradient_kernel, jax.ShapeDtypeStruct((planes, share, width), BF16), 1_000_000, 1_200_000)(
        parts, resid
    )
    gradient = lax.all_to_all(copies, COLUMN, 0, 0, tiled=True).reshape(count, width)
    spread = call(spread_kernel, jax.ShapeDtypeStruct((blocks, row_lines, LANES), BF16), 600_000_000, 6_000_000)(
        hot, gradient
    )
    grad_in = lax.all_to_all(spread, PLANE, 0, 0, tiled=True)
    scored, totals = call(
        project_kernel,
        (
            jax.ShapeDtypeStruct((blocks, code_lines, LANES), BF16),
            jax.ShapeDtypeStruct((layers, REQUESTS, panel), F32),
        ),
        1_300_000_000,
        8_000_000,
        [pltpu.VMEM((layers, blocks * CAP, panel), F32)],
    )(grad_in, codes_in, decoder)
    scores_in = lax.all_to_all(scored, TOK, 0, 0, tiled=True)
    placed = call(place_kernel, jax.ShapeDtypeStruct((layers, rows, panel), BF16), 140_000_000, 1_000_000)(
        slot, scores_in
    )
    scores = placed.reshape(layers, kact, count, panel).transpose(0, 2, 1, 3)
    return scores, totals.transpose(1, 0, 2)


def solution(mesh):
    fine = Mesh(mesh.devices.reshape(4, 4, 2, 2, 4), EVERY)
    placed = (
        P(LYR, TOK, None, None),
        P(LYR, TOK, None),
        P(TOK),
        P(TOK),
        P(TOK, None),
        P(LYR, TOK, None),
    )
    return jax.shard_map(
        per_device,
        mesh=fine,
        in_specs=placed,
        out_specs=(P(LYR, TOK, None, None), P(None, LYR, TOK)),
        check_vma=False,
    )
```

```python
import jax
import jax.numpy as jnp
from jax import lax
from jax.experimental import pallas as pl
from jax.experimental.pallas import tpu as pltpu
from jax.sharding import Mesh, PartitionSpec as P

PANELS = 32
REQUESTS = 16
CAP = 16
LANES = 128
TOK = ("zh", "x", "c")
SPREAD = ("x", "zh", "c")
LYR = ("zl", "y")
PLANE = ("x", "y", "c")
COLUMN = ("zl", "zh")
EVERY = ("zh", "x", "c", "zl", "y")
BF16 = jnp.bfloat16
F32 = jnp.float32


def call(kernel, out_shape, flops, moved, scratch=(), limit=10):
    return pl.pallas_call(
        kernel,
        out_shape=out_shape,
        scratch_shapes=list(scratch),
        compiler_params=pltpu.CompilerParams(vmem_limit_bytes=limit * 1024 * 1024),
        cost_estimate=pl.CostEstimate(flops=flops, bytes_accessed=moved, transcendentals=0),
    )


def iota(shape, axis):
    return lax.broadcasted_iota(jnp.int32, shape, axis)


def to_column(row):
    n = row.shape[1]
    diag = iota((n, n), 0) == iota((n, n), 1)
    return jnp.sum(jnp.where(diag, jnp.broadcast_to(row, (n, n)), jnp.zeros((n, n), row.dtype)), axis=1, keepdims=True)


def lane_groups(info):
    groups = info.shape[0]
    return jnp.sum(info.reshape(groups // 4, 4, 1, LANES), axis=1)


def pack_kernel(small_ref, codes_ref, out_ref, slot_ref):
    layers, rows, panel = codes_ref.shape
    tokens = small_ref.shape[1]
    kact = rows // tokens
    first_layer = lax.axis_index(LYR) * layers
    slots = layers * CAP
    per = LANES // slots
    halves = panel // LANES
    target = small_ref[layers * kact : layers * kact + 1, :]
    request = small_ref[layers * kact + 1 : layers * kact + 2, :].astype(F32) + 1.0
    target_row = jnp.concatenate([target] * kact, axis=1)
    request_row = jnp.concatenate([request] * kact, axis=1)
    token_row = (iota((1, rows), 1) % tokens + 1).astype(F32)
    token_info = jnp.zeros((PANELS, LANES), F32)
    request_info = jnp.zeros((PANELS, LANES), F32)
    for l in range(layers):
        panel_id = jnp.concatenate([small_ref[l * kact + k : l * kact + k + 1, :] for k in range(kact)], axis=1)
        zh, x, c = panel_id // 8, panel_id // 2 % 4, panel_id % 2
        ids_row = (x * 8 + zh * 2 + c).astype(F32)
        ids_col = to_column(ids_row)
        earlier = (ids_col == ids_row) & (iota((rows, rows), 0) < iota((rows, rows), 1))
        rank = jnp.sum(jnp.where(earlier, 1.0, 0.0), axis=0, keepdims=True)
        alive = target_row >= first_layer + l
        slot = jnp.where(alive, (ids_row * CAP + rank).astype(jnp.int32), -1)
        slot_ref[l : l + 1, :] = slot
        pick = jnp.where(iota((PANELS * CAP, rows), 0) == slot, 1.0, 0.0).astype(BF16)
        sent = jnp.dot(pick, codes_ref[l], preferred_element_type=F32).astype(BF16)
        for h in range(halves):
            half = sent[:, h * LANES : (h + 1) * LANES]
            out_ref[:, h * slots + l * CAP : h * slots + (l + 1) * CAP, :] = half.reshape(PANELS, CAP, LANES)
        named = (iota((PANELS, rows), 0).astype(F32) == ids_row) & alive
        place = jnp.where(iota((rows, LANES), 1) % slots == to_column(rank).astype(jnp.int32) + l * CAP, 1.0, 0.0)
        place = place.astype(BF16)
        token_info += jnp.dot(jnp.where(named, token_row, 0.0).astype(BF16), place, preferred_element_type=F32)
        request_info += jnp.dot(jnp.where(named, request_row, 0.0).astype(BF16), place, preferred_element_type=F32)
    spot = iota((PANELS, LANES), 1) // slots
    sender = lax.axis_index("y") % 2 * 2 + iota((PANELS, LANES), 0) % 2
    token_info = jnp.where(spot == sender, token_info, 0.0)
    request_info = jnp.where(spot == lax.axis_index(SPREAD) % per, request_info, 0.0)
    line = iota((PANELS, 8, LANES), 1)
    tile = jnp.where(
        line == 0,
        token_info.reshape(PANELS, 1, LANES),
        jnp.where(line == 1, request_info.reshape(PANELS, 1, LANES), 0.0),
    )
    out_ref[:, halves * slots : halves * slots + 8, :] = tile.astype(BF16)


def build_kernel(codes_ref, weight_ref, out_ref):
    blocks = codes_ref.shape[0]
    layers, panel, width = weight_ref.shape
    slots = layers * CAP
    halves = panel // LANES
    step = 2 * LANES
    for l in range(layers):
        codes = jnp.concatenate(
            [
                codes_ref[:, h * slots + l * CAP : h * slots + (l + 1) * CAP, :].reshape(blocks * CAP, LANES)
                for h in range(halves)
            ],
            axis=1,
        )
        for n in range(0, width, step):
            built = jnp.dot(codes, weight_ref[l, :, n : n + step], preferred_element_type=F32).astype(BF16)
            for i in range(0, step, LANES):
                at = (n + i) // LANES * slots + l * CAP
                out_ref[:, at : at + CAP, :] = built[:, i : i + LANES].reshape(blocks, CAP, LANES)
    end = width // LANES * slots
    out_ref[:, end : end + 8, :] = codes_ref[:, halves * slots : halves * slots + 8, :]


def reduce_kernel(rows_ref, resid_ref, out_ref, hot_ref):
    groups = rows_ref.shape[0]
    tokens, width = out_ref.shape
    count = hot_ref.shape[0]
    slots = count // groups
    step = 2 * LANES
    end = width // LANES * slots
    token = lane_groups(rows_ref[:, end : end + 8, :].astype(F32)[:, 0:1, :])
    want = (iota((tokens, LANES), 0) + 1).astype(F32)
    hot_t = jnp.concatenate([jnp.where(token[g] == want, 1.0, 0.0) for g in range(count // LANES)], axis=1)
    hot_ref[...] = hot_t.T.astype(BF16)
    hot_t = hot_t.astype(BF16)
    home = (lax.axis_index("zh") == lax.axis_index("y")) & (lax.axis_index("zl") == 0)
    share = jnp.where(home, 1.0, 0.0)
    for n in range(0, width, step):
        rows = jnp.concatenate(
            [
                rows_ref[:, (n + i) // LANES * slots : (n + i) // LANES * slots + slots, :].reshape(count, LANES)
                for i in range(0, step, LANES)
            ],
            axis=1,
        )
        summed = jnp.dot(hot_t, rows, preferred_element_type=F32)
        out_ref[:, n : n + step] = (summed - share * resid_ref[:, n : n + step].astype(F32)).astype(out_ref.dtype)


def gradient_kernel(parts_ref, out_ref):
    planes, tokens, width = parts_ref.shape
    missing = parts_ref[0].astype(F32)
    for i in range(1, planes):
        missing = missing + parts_ref[i].astype(F32)
    error = -missing
    spread = jnp.sum(error * error, axis=-1, keepdims=True) * (1.0 / width)
    gradient = (error * lax.rsqrt(spread + 1e-06)).astype(BF16)
    for i in range(planes):
        out_ref[i] = gradient


def spread_kernel(hot_ref, gradient_ref, out_ref):
    groups = out_ref.shape[0]
    count = hot_ref.shape[0]
    width = gradient_ref.shape[1]
    slots = count // groups
    step = 2 * LANES
    for n in range(0, width, step):
        rows = jnp.dot(hot_ref[...], gradient_ref[:, n : n + step], preferred_element_type=F32).astype(BF16)
        for i in range(0, step, LANES):
            at = (n + i) // LANES * slots
            out_ref[:, at : at + slots, :] = rows[:, i : i + LANES].reshape(groups, slots, LANES)


def project_kernel(rows_ref, codes_ref, weight_ref, score_ref, total_ref):
    blocks = rows_ref.shape[0]
    layers, panel, width = weight_ref.shape
    slots = layers * CAP
    halves = panel // LANES
    projections = []
    for l in range(layers):
        rows = jnp.concatenate(
            [
                rows_ref[:, n * slots + l * CAP : n * slots + (l + 1) * CAP, :].reshape(blocks * CAP, LANES)
                for n in range(width // LANES)
            ],
            axis=1,
        )
        projections.append(
            lax.dot_general(rows, weight_ref[l], (((1,), (1,)), ((), ())), preferred_element_type=F32).astype(BF16)
        )
    request = lane_groups(codes_ref[:, halves * slots : halves * slots + 8, :].astype(F32)[:, 1:2, :])
    lane_layer = iota((layers * REQUESTS, LANES), 1) % slots // CAP
    line = iota((layers * REQUESTS, LANES), 0)
    want = (line % REQUESTS + 1).astype(F32)
    here = lane_layer == line // REQUESTS
    member = jnp.concatenate(
        [jnp.where((request[g] == want) & here, 1.0, 0.0) for g in range(blocks * slots // LANES)], axis=1
    ).astype(BF16)
    for h in range(halves):
        values = []
        for l in range(layers):
            at = slice(h * slots + l * CAP, h * slots + (l + 1) * CAP)
            codes = codes_ref[:, at, :].reshape(blocks * CAP, LANES).astype(F32)
            projected = projections[l][:, h * LANES : (h + 1) * LANES].astype(F32)
            value = codes * projected
            score_ref[:, at, :] = value.astype(BF16).reshape(blocks, CAP, LANES)
            values.append(value.reshape(blocks, CAP, LANES))
        value = jnp.concatenate(values, axis=1).reshape(blocks * slots, LANES)
        upper = value.astype(BF16)
        lower = (value - upper.astype(F32)).astype(BF16)
        summed = jnp.dot(member, upper, preferred_element_type=F32) + jnp.dot(
            member, lower, preferred_element_type=F32
        )
        for l in range(layers):
            total_ref[:, l, h * LANES : (h + 1) * LANES] = summed[l * REQUESTS : (l + 1) * REQUESTS]


def place_kernel(slot_ref, scores_ref, out_ref):
    layers, rows = slot_ref.shape
    slots = layers * CAP
    halves = out_ref.shape[2] // LANES
    for l in range(layers):
        column = to_column(slot_ref[l : l + 1, :])
        pick = jnp.where(iota((rows, PANELS * CAP), 1) == column, 1.0, 0.0).astype(BF16)
        scores = jnp.concatenate(
            [
                scores_ref[:, h * slots + l * CAP : h * slots + (l + 1) * CAP, :].reshape(PANELS * CAP, LANES)
                for h in range(halves)
            ],
            axis=1,
        )
        out_ref[l] = jnp.dot(pick, scores, preferred_element_type=F32).astype(BF16)


def per_device(feature_codes, block_ids, target_layer, request_ids, target_resid, decoder):
    layers, count, kact, panel = feature_codes.shape
    width = target_resid.shape[1]
    rows = count * kact
    blocks = lax.axis_size(TOK)
    planes = lax.axis_size(COLUMN)
    share = count // planes
    slots = layers * CAP
    code_lines = panel // LANES * slots
    row_lines = width // LANES * slots
    small = jnp.concatenate(
        [
            block_ids.transpose(0, 2, 1).reshape(layers * kact, count),
            target_layer.reshape(1, count),
            request_ids.reshape(1, count),
        ],
        axis=0,
    )
    codes = feature_codes.transpose(0, 2, 1, 3).reshape(layers, rows, panel)
    sent, slot = call(
        pack_kernel,
        (
            jax.ShapeDtypeStruct((blocks, code_lines + 8, LANES), BF16),
            jax.ShapeDtypeStruct((layers, rows), jnp.int32),
        ),
        300_000_000,
        4_000_000,
    )(small, codes)
    codes_in = lax.all_to_all(sent, SPREAD, 0, 0, tiled=True)

    built = call(
        build_kernel, jax.ShapeDtypeStruct((blocks, row_lines + 8, LANES), BF16), 1_200_000_000, 8_000_000
    )(codes_in, decoder)
    rows_in = lax.all_to_all(built, PLANE, 0, 0, tiled=True)
    partial, hot = call(
        reduce_kernel,
        (jax.ShapeDtypeStruct((count, width), BF16), jax.ShapeDtypeStruct((blocks * slots, count), BF16)),
        600_000_000,
        6_000_000,
    )(rows_in, target_resid)
    parts = lax.all_to_all(partial.reshape(planes, share, width), COLUMN, 0, 0, tiled=True)
    copies = call(gradient_kernel, jax.ShapeDtypeStruct((planes, share, width), BF16), 1_000_000, 1_200_000)(
        parts
    )
    gradient = lax.all_to_all(copies, COLUMN, 0, 0, tiled=True).reshape(count, width)
    spread = call(spread_kernel, jax.ShapeDtypeStruct((blocks, row_lines, LANES), BF16), 600_000_000, 6_000_000)(
        hot, gradient
    )
    grad_in = lax.all_to_all(spread, PLANE, 0, 0, tiled=True)
    scored, totals = call(
        project_kernel,
        (
            jax.ShapeDtypeStruct((blocks, code_lines, LANES), BF16),
            jax.ShapeDtypeStruct((REQUESTS, layers, panel), F32),
        ),
        1_300_000_000,
        8_000_000,
    )(grad_in, codes_in, decoder)
    scores_in = lax.all_to_all(scored, SPREAD, 0, 0, tiled=True)
    placed = call(place_kernel, jax.ShapeDtypeStruct((layers, rows, panel), BF16), 140_000_000, 1_000_000)(
        slot, scores_in
    )
    scores = placed.reshape(layers, kact, count, panel).transpose(0, 2, 1, 3)
    return scores, totals


def solution(mesh):
    fine = Mesh(mesh.devices.reshape(4, 4, 2, 2, 4), EVERY)
    placed = (
        P(LYR, TOK, None, None),
        P(LYR, TOK, None),
        P(TOK),
        P(TOK),
        P(TOK, None),
        P(LYR, TOK, None),
    )
    return jax.shard_map(
        per_device,
        mesh=fine,
        in_specs=placed,
        out_specs=(P(LYR, TOK, None, None), P(None, LYR, TOK)),
        check_vma=False,
    )
```

```python
import jax
import jax.numpy as jnp
from jax import lax
from jax.experimental import pallas as pl
from jax.experimental.pallas import tpu as pltpu
from jax.sharding import Mesh, PartitionSpec as P

PANELS = 32
REQUESTS = 16
CAP = 16
LANES = 128
TOK = ("zh", "x", "c")
SPREAD = ("x", "zh", "c")
LYR = ("zl", "y")
PLANE = ("x", "y", "c")
COLUMN = ("zl", "zh")
EVERY = ("zh", "x", "c", "zl", "y")
BF16 = jnp.bfloat16
F32 = jnp.float32


def call(kernel, out_shape, flops, moved, scratch=(), limit=10):
    return pl.pallas_call(
        kernel,
        out_shape=out_shape,
        scratch_shapes=list(scratch),
        compiler_params=pltpu.CompilerParams(vmem_limit_bytes=limit * 1024 * 1024),
        cost_estimate=pl.CostEstimate(flops=flops, bytes_accessed=moved, transcendentals=0),
    )


def iota(shape, axis):
    return lax.broadcasted_iota(jnp.int32, shape, axis)


def to_column(row):
    n = row.shape[1]
    diag = iota((n, n), 0) == iota((n, n), 1)
    return jnp.sum(jnp.where(diag, jnp.broadcast_to(row, (n, n)), jnp.zeros((n, n), row.dtype)), axis=1, keepdims=True)


def lane_groups(info):
    groups = info.shape[0]
    return jnp.sum(info.reshape(groups // 4, 4, 1, LANES), axis=1)


def pack_kernel(
    ids_hbm, target_hbm, request_hbm, codes_hbm, weight_hbm,
    out_ref, slot_ref, weight_out,
    ids_ref, target_ref, request_ref, codes_ref, sems,
):
    pairs = (
        (ids_hbm, ids_ref), (target_hbm, target_ref), (request_hbm, request_ref), (codes_hbm, codes_ref),
        (weight_hbm, weight_out),
    )
    loads = [pltpu.make_async_copy(source, held, sems.at[i]) for i, (source, held) in enumerate(pairs)]
    for load in loads:
        load.start()
    for load in loads[:-2]:
        load.wait()
    layers, tokens, kact, panel = codes_ref.shape
    rows = kact * tokens
    first_layer = lax.axis_index(LYR) * layers
    slots = layers * CAP
    per = LANES // slots
    halves = panel // LANES
    small = jnp.concatenate([ids_ref[l] for l in range(layers)] + [target_ref[...], request_ref[...]], axis=0)
    small = small.astype(F32).astype(BF16)
    spaced = [
        jnp.dot(
            small,
            jnp.where(iota((tokens, rows), 1) == iota((tokens, rows), 0) * kact + k, 1.0, 0.0).astype(BF16),
            preferred_element_type=F32,
        )
        for k in range(kact)
    ]
    at = layers * kact
    target_row = sum(part[at : at + 1] for part in spaced).astype(jnp.int32)
    request_row = sum(part[at + 1 : at + 2] for part in spaced) + 1.0
    token_row = (iota((1, rows), 1) // kact + 1).astype(F32)
    loads[-2].wait()
    token_info = jnp.zeros((PANELS, LANES), F32)
    request_info = jnp.zeros((PANELS, LANES), F32)
    for l in range(layers):
        panel_id = sum(spaced[k][l * kact + k : l * kact + k + 1] for k in range(kact)).astype(jnp.int32)
        zh, x, c = panel_id // 8, panel_id // 2 % 4, panel_id % 2
        ids_row = (x * 8 + zh * 2 + c).astype(F32)
        ids_col = to_column(ids_row)
        earlier = (ids_col == ids_row) & (iota((rows, rows), 0) < iota((rows, rows), 1))
        rank = jnp.sum(jnp.where(earlier, 1.0, 0.0), axis=0, keepdims=True)
        alive = target_row >= first_layer + l
        slot = jnp.where(alive, (ids_row * CAP + rank).astype(jnp.int32), -1)
        slot_ref[l : l + 1, :] = slot
        pick = jnp.where(iota((PANELS * CAP, rows), 0) == slot, 1.0, 0.0).astype(BF16)
        sent = jnp.dot(pick, codes_ref[l].reshape(rows, panel), preferred_element_type=F32).astype(BF16)
        for h in range(halves):
            half = sent[:, h * LANES : (h + 1) * LANES]
            out_ref[:, h * slots + l * CAP : h * slots + (l + 1) * CAP, :] = half.reshape(PANELS, CAP, LANES)
        named = (iota((PANELS, rows), 0).astype(F32) == ids_row) & alive
        place = jnp.where(iota((rows, LANES), 1) % slots == to_column(rank).astype(jnp.int32) + l * CAP, 1.0, 0.0)
        place = place.astype(BF16)
        token_info += jnp.dot(jnp.where(named, token_row, 0.0).astype(BF16), place, preferred_element_type=F32)
        request_info += jnp.dot(jnp.where(named, request_row, 0.0).astype(BF16), place, preferred_element_type=F32)
    spot = iota((PANELS, LANES), 1) // slots
    sender = lax.axis_index("y") % 2 * 2 + iota((PANELS, LANES), 0) % 2
    token_info = jnp.where(spot == sender, token_info, 0.0)
    request_info = jnp.where(spot == lax.axis_index(SPREAD) % per, request_info, 0.0)
    line = iota((PANELS, 8, LANES), 1)
    tile = jnp.where(
        line == 0,
        token_info.reshape(PANELS, 1, LANES),
        jnp.where(line == 1, request_info.reshape(PANELS, 1, LANES), 0.0),
    )
    out_ref[:, halves * slots : halves * slots + 8, :] = tile.astype(BF16)
    loads[-1].wait()


def build_kernel(codes_ref, weight_ref, out_ref):
    blocks = codes_ref.shape[0]
    layers, panel, width = weight_ref.shape
    slots = layers * CAP
    halves = panel // LANES
    step = 2 * LANES
    for l in range(layers):
        codes = jnp.concatenate(
            [
                codes_ref[:, h * slots + l * CAP : h * slots + (l + 1) * CAP, :].reshape(blocks * CAP, LANES)
                for h in range(halves)
            ],
            axis=1,
        )
        for n in range(0, width, step):
            built = jnp.dot(codes, weight_ref[l, :, n : n + step], preferred_element_type=F32).astype(BF16)
            for i in range(0, step, LANES):
                at = (n + i) // LANES * slots + l * CAP
                out_ref[:, at : at + CAP, :] = built[:, i : i + LANES].reshape(blocks, CAP, LANES)
    end = width // LANES * slots
    out_ref[:, end : end + 8, :] = codes_ref[:, halves * slots : halves * slots + 8, :]


def reduce_kernel(rows_ref, resid_ref, out_ref, hot_ref):
    groups = rows_ref.shape[0]
    tokens, width = out_ref.shape
    count = hot_ref.shape[0]
    slots = count // groups
    step = 2 * LANES
    end = width // LANES * slots
    token = lane_groups(rows_ref[:, end : end + 8, :].astype(F32)[:, 0:1, :])
    want = (iota((tokens, LANES), 0) + 1).astype(F32)
    hot_t = jnp.concatenate([jnp.where(token[g] == want, 1.0, 0.0) for g in range(count // LANES)], axis=1)
    hot_ref[...] = hot_t.T.astype(BF16)
    hot_t = hot_t.astype(BF16)
    home = (lax.axis_index("zh") == lax.axis_index("y")) & (lax.axis_index("zl") == 0)
    share = jnp.where(home, 1.0, 0.0)
    for n in range(0, width, step):
        rows = jnp.concatenate(
            [
                rows_ref[:, (n + i) // LANES * slots : (n + i) // LANES * slots + slots, :].reshape(count, LANES)
                for i in range(0, step, LANES)
            ],
            axis=1,
        )
        summed = jnp.dot(hot_t, rows, preferred_element_type=F32)
        out_ref[:, n : n + step] = (summed - share * resid_ref[:, n : n + step].astype(F32)).astype(out_ref.dtype)


def gradient_kernel(parts_ref, out_ref):
    planes, tokens, width = parts_ref.shape
    missing = parts_ref[0].astype(F32)
    for i in range(1, planes):
        missing = missing + parts_ref[i].astype(F32)
    error = -missing
    spread = jnp.sum(error * error, axis=-1, keepdims=True) * (1.0 / width)
    gradient = (error * lax.rsqrt(spread + 1e-06)).astype(BF16)
    for i in range(planes):
        out_ref[i] = gradient


def spread_kernel(hot_ref, gradient_ref, out_ref):
    groups = out_ref.shape[0]
    count = hot_ref.shape[0]
    width = gradient_ref.shape[1]
    slots = count // groups
    step = 2 * LANES
    for n in range(0, width, step):
        rows = jnp.dot(hot_ref[...], gradient_ref[:, n : n + step], preferred_element_type=F32).astype(BF16)
        for i in range(0, step, LANES):
            at = (n + i) // LANES * slots
            out_ref[:, at : at + slots, :] = rows[:, i : i + LANES].reshape(groups, slots, LANES)


def project_kernel(rows_ref, codes_ref, weight_ref, score_ref, total_ref):
    blocks = rows_ref.shape[0]
    layers, panel, width = weight_ref.shape
    slots = layers * CAP
    halves = panel // LANES
    projections = []
    for l in range(layers):
        rows = jnp.concatenate(
            [
                rows_ref[:, n * slots + l * CAP : n * slots + (l + 1) * CAP, :].reshape(blocks * CAP, LANES)
                for n in range(width // LANES)
            ],
            axis=1,
        )
        projections.append(
            lax.dot_general(rows, weight_ref[l], (((1,), (1,)), ((), ())), preferred_element_type=F32).astype(BF16)
        )
    request = lane_groups(codes_ref[:, halves * slots : halves * slots + 8, :].astype(F32)[:, 1:2, :])
    lane_layer = iota((layers * REQUESTS, LANES), 1) % slots // CAP
    line = iota((layers * REQUESTS, LANES), 0)
    want = (line % REQUESTS + 1).astype(F32)
    here = lane_layer == line // REQUESTS
    member = jnp.concatenate(
        [jnp.where((request[g] == want) & here, 1.0, 0.0) for g in range(blocks * slots // LANES)], axis=1
    ).astype(BF16)
    for h in range(halves):
        values = []
        for l in range(layers):
            at = slice(h * slots + l * CAP, h * slots + (l + 1) * CAP)
            codes = codes_ref[:, at, :].reshape(blocks * CAP, LANES).astype(F32)
            projected = projections[l][:, h * LANES : (h + 1) * LANES].astype(F32)
            value = codes * projected
            score_ref[:, at, :] = value.astype(BF16).reshape(blocks, CAP, LANES)
            values.append(value.reshape(blocks, CAP, LANES))
        value = jnp.concatenate(values, axis=1).reshape(blocks * slots, LANES)
        upper = value.astype(BF16)
        lower = (value - upper.astype(F32)).astype(BF16)
        summed = jnp.dot(member, upper, preferred_element_type=F32) + jnp.dot(
            member, lower, preferred_element_type=F32
        )
        for l in range(layers):
            total_ref[:, l, h * LANES : (h + 1) * LANES] = summed[l * REQUESTS : (l + 1) * REQUESTS]


def place_kernel(slot_ref, scores_ref, out_ref):
    layers, rows = slot_ref.shape
    slots = layers * CAP
    halves = out_ref.shape[3] // LANES
    for l in range(layers):
        column = to_column(slot_ref[l : l + 1, :])
        pick = jnp.where(iota((rows, PANELS * CAP), 1) == column, 1.0, 0.0).astype(BF16)
        scores = jnp.concatenate(
            [
                scores_ref[:, h * slots + l * CAP : h * slots + (l + 1) * CAP, :].reshape(PANELS * CAP, LANES)
                for h in range(halves)
            ],
            axis=1,
        )
        placed = jnp.dot(pick, scores, preferred_element_type=F32).astype(BF16)
        out_ref[l] = placed.reshape(out_ref.shape[1:])


def per_device(feature_codes, block_ids, target_layer, request_ids, target_resid, decoder):
    layers, count, kact, panel = feature_codes.shape
    width = target_resid.shape[1]
    rows = count * kact
    blocks = lax.axis_size(TOK)
    planes = lax.axis_size(COLUMN)
    share = count // planes
    slots = layers * CAP
    code_lines = panel // LANES * slots
    row_lines = width // LANES * slots
    offchip = pl.BlockSpec(memory_space=pltpu.HBM)
    onchip = pl.BlockSpec(memory_space=pltpu.VMEM)
    held = (
        block_ids.transpose(0, 2, 1),
        target_layer.reshape(1, count),
        request_ids.reshape(1, count),
        feature_codes,
        decoder,
    )
    sent, slot, weights = pl.pallas_call(
        pack_kernel,
        out_shape=(
            jax.ShapeDtypeStruct((blocks, code_lines + 8, LANES), BF16),
            jax.ShapeDtypeStruct((layers, rows), jnp.int32),
            jax.ShapeDtypeStruct(decoder.shape, decoder.dtype),
        ),
        in_specs=[offchip] * len(held),
        out_specs=(onchip, onchip, pl.BlockSpec(memory_space=pl.ANY)),
        scratch_shapes=[pltpu.VMEM(a.shape, a.dtype) for a in held[:-1]] + [pltpu.SemaphoreType.DMA((len(held),))],
        compiler_params=pltpu.CompilerParams(vmem_limit_bytes=10 * 1024 * 1024),
        cost_estimate=pl.CostEstimate(flops=300_000_000, bytes_accessed=4_000_000, transcendentals=0),
    )(*[pltpu.with_memory_space_constraint(a, pltpu.HBM) for a in held])
    codes_in = lax.all_to_all(sent, SPREAD, 0, 0, tiled=True)

    built = call(
        build_kernel, jax.ShapeDtypeStruct((blocks, row_lines + 8, LANES), BF16), 1_200_000_000, 8_000_000
    )(codes_in, weights)
    rows_in = lax.all_to_all(built, PLANE, 0, 0, tiled=True)
    partial, hot = call(
        reduce_kernel,
        (jax.ShapeDtypeStruct((count, width), BF16), jax.ShapeDtypeStruct((blocks * slots, count), BF16)),
        600_000_000,
        6_000_000,
    )(rows_in, target_resid)
    parts = lax.all_to_all(partial.reshape(planes, share, width), COLUMN, 0, 0, tiled=True)
    copies = call(gradient_kernel, jax.ShapeDtypeStruct((planes, share, width), BF16), 1_000_000, 1_200_000)(
        parts
    )
    gradient = lax.all_to_all(copies, COLUMN, 0, 0, tiled=True).reshape(count, width)
    spread = call(spread_kernel, jax.ShapeDtypeStruct((blocks, row_lines, LANES), BF16), 600_000_000, 6_000_000)(
        hot, gradient
    )
    grad_in = lax.all_to_all(spread, PLANE, 0, 0, tiled=True)
    scored, totals = call(
        project_kernel,
        (
            jax.ShapeDtypeStruct((blocks, code_lines, LANES), BF16),
            jax.ShapeDtypeStruct((REQUESTS, layers, panel), F32),
        ),
        1_300_000_000,
        8_000_000,
    )(grad_in, codes_in, weights)
    scores_in = lax.all_to_all(scored, SPREAD, 0, 0, tiled=True)
    scores = call(place_kernel, jax.ShapeDtypeStruct(feature_codes.shape, BF16), 140_000_000, 1_000_000)(
        slot, scores_in
    )
    return scores, totals


def solution(mesh):
    fine = Mesh(mesh.devices.reshape(4, 4, 2, 2, 4), EVERY)
    placed = (
        P(LYR, TOK, None, None),
        P(LYR, TOK, None),
        P(TOK),
        P(TOK),
        P(TOK, None),
        P(LYR, TOK, None),
    )
    return jax.shard_map(
        per_device,
        mesh=fine,
        in_specs=placed,
        out_specs=(P(LYR, TOK, None, None), P(None, LYR, TOK)),
        check_vma=False,
    )
```

```python
import jax
import jax.numpy as jnp
from jax import lax
from jax.experimental import pallas as pl
from jax.experimental.pallas import tpu as pltpu
from jax.sharding import Mesh, PartitionSpec as P

PANELS = 32
REQUESTS = 16
CAP = 16
LANES = 128
TOK = ("zh", "x", "c")
SPREAD = ("x", "c", "zh")
LYR = ("zl", "y")
PLANE = ("x", "c", "y")
COLUMN = ("zl", "zh")
EVERY = ("zh", "x", "c", "zl", "y")
BF16 = jnp.bfloat16
F32 = jnp.float32


def call(kernel, out_shape, flops, moved, scratch=(), limit=10):
    return pl.pallas_call(
        kernel,
        out_shape=out_shape,
        scratch_shapes=list(scratch),
        compiler_params=pltpu.CompilerParams(vmem_limit_bytes=limit * 1024 * 1024),
        cost_estimate=pl.CostEstimate(flops=flops, bytes_accessed=moved, transcendentals=0),
    )


def iota(shape, axis):
    return lax.broadcasted_iota(jnp.int32, shape, axis)


def to_column(row):
    n = row.shape[1]
    diag = iota((n, n), 0) == iota((n, n), 1)
    return jnp.sum(jnp.where(diag, jnp.broadcast_to(row, (n, n)), jnp.zeros((n, n), row.dtype)), axis=1, keepdims=True)


def lane_groups(info):
    groups = info.shape[0]
    return jnp.sum(info.reshape(groups // 4, 4, 1, LANES), axis=1)


def pack_kernel(
    ids_hbm, target_hbm, request_hbm, codes_hbm, weight_hbm,
    out_ref, slot_ref, weight_out,
    ids_ref, target_ref, request_ref, codes_ref, sems,
):
    pairs = (
        (ids_hbm, ids_ref), (target_hbm, target_ref), (request_hbm, request_ref), (codes_hbm, codes_ref),
        (weight_hbm, weight_out),
    )
    loads = [pltpu.make_async_copy(source, held, sems.at[i]) for i, (source, held) in enumerate(pairs)]
    for load in loads:
        load.start()
    for load in loads[:-2]:
        load.wait()
    layers, tokens, kact, panel = codes_ref.shape
    rows = kact * tokens
    first_layer = lax.axis_index(LYR) * layers
    slots = layers * CAP
    per = LANES // slots
    halves = panel // LANES
    small = jnp.concatenate([ids_ref[l] for l in range(layers)] + [target_ref[...], request_ref[...]], axis=0)
    small = small.astype(F32).astype(BF16)
    spaced = [
        jnp.dot(
            small,
            jnp.where(iota((tokens, rows), 1) == iota((tokens, rows), 0) * kact + k, 1.0, 0.0).astype(BF16),
            preferred_element_type=F32,
        )
        for k in range(kact)
    ]
    at = layers * kact
    target_row = sum(part[at : at + 1] for part in spaced).astype(jnp.int32)
    request_row = sum(part[at + 1 : at + 2] for part in spaced) + 1.0
    token_row = (iota((1, rows), 1) // kact + 1).astype(F32)
    loads[-2].wait()
    token_info = jnp.zeros((PANELS, LANES), F32)
    request_info = jnp.zeros((PANELS, LANES), F32)
    for l in range(layers):
        panel_id = sum(spaced[k][l * kact + k : l * kact + k + 1] for k in range(kact)).astype(jnp.int32)
        zh, x, c = panel_id // 8, panel_id // 2 % 4, panel_id % 2
        ids_row = (x * 8 + c * 4 + zh).astype(F32)
        ids_col = to_column(ids_row)
        earlier = (ids_col == ids_row) & (iota((rows, rows), 0) < iota((rows, rows), 1))
        rank = jnp.sum(jnp.where(earlier, 1.0, 0.0), axis=0, keepdims=True)
        alive = target_row >= first_layer + l
        slot = jnp.where(alive, (ids_row * CAP + rank).astype(jnp.int32), -1)
        slot_ref[l : l + 1, :] = slot
        pick = jnp.where(iota((PANELS * CAP, rows), 0) == slot, 1.0, 0.0).astype(BF16)
        sent = jnp.dot(pick, codes_ref[l].reshape(rows, panel), preferred_element_type=F32).astype(BF16)
        for h in range(halves):
            half = sent[:, h * LANES : (h + 1) * LANES]
            out_ref[:, h * slots + l * CAP : h * slots + (l + 1) * CAP, :] = half.reshape(PANELS, CAP, LANES)
        named = (iota((PANELS, rows), 0).astype(F32) == ids_row) & alive
        place = jnp.where(iota((rows, LANES), 1) % slots == to_column(rank).astype(jnp.int32) + l * CAP, 1.0, 0.0)
        place = place.astype(BF16)
        token_info += jnp.dot(jnp.where(named, token_row, 0.0).astype(BF16), place, preferred_element_type=F32)
        request_info += jnp.dot(jnp.where(named, request_row, 0.0).astype(BF16), place, preferred_element_type=F32)
    spot = iota((PANELS, LANES), 1) // slots
    token_info = jnp.where(spot == lax.axis_index("y") % per, token_info, 0.0)
    request_info = jnp.where(spot == lax.axis_index(SPREAD) % per, request_info, 0.0)
    line = iota((PANELS, 8, LANES), 1)
    tile = jnp.where(
        line == 0,
        token_info.reshape(PANELS, 1, LANES),
        jnp.where(line == 1, request_info.reshape(PANELS, 1, LANES), 0.0),
    )
    out_ref[:, halves * slots : halves * slots + 8, :] = tile.astype(BF16)
    loads[-1].wait()


def build_kernel(codes_ref, weight_ref, out_ref):
    blocks = codes_ref.shape[0]
    layers, panel, width = weight_ref.shape
    slots = layers * CAP
    halves = panel // LANES
    step = 2 * LANES
    for l in range(layers):
        codes = jnp.concatenate(
            [
                codes_ref[:, h * slots + l * CAP : h * slots + (l + 1) * CAP, :].reshape(blocks * CAP, LANES)
                for h in range(halves)
            ],
            axis=1,
        )
        for n in range(0, width, step):
            built = jnp.dot(codes, weight_ref[l, :, n : n + step], preferred_element_type=F32).astype(BF16)
            for i in range(0, step, LANES):
                at = (n + i) // LANES * slots + l * CAP
                out_ref[:, at : at + CAP, :] = built[:, i : i + LANES].reshape(blocks, CAP, LANES)
    end = width // LANES * slots
    out_ref[:, end : end + 8, :] = codes_ref[:, halves * slots : halves * slots + 8, :]


def reduce_kernel(rows_ref, resid_ref, out_ref, hot_ref):
    groups = rows_ref.shape[0]
    tokens, width = out_ref.shape
    count = hot_ref.shape[0]
    slots = count // groups
    step = 2 * LANES
    end = width // LANES * slots
    token = lane_groups(rows_ref[:, end : end + 8, :].astype(F32)[:, 0:1, :])
    want = (iota((tokens, LANES), 0) + 1).astype(F32)
    hot_t = jnp.concatenate([jnp.where(token[g] == want, 1.0, 0.0) for g in range(count // LANES)], axis=1)
    hot_ref[...] = hot_t.T.astype(BF16)
    hot_t = hot_t.astype(BF16)
    home = (lax.axis_index("zh") == lax.axis_index("y")) & (lax.axis_index("zl") == 0)
    share = jnp.where(home, 1.0, 0.0)
    for n in range(0, width, step):
        rows = jnp.concatenate(
            [
                rows_ref[:, (n + i) // LANES * slots : (n + i) // LANES * slots + slots, :].reshape(count, LANES)
                for i in range(0, step, LANES)
            ],
            axis=1,
        )
        summed = jnp.dot(hot_t, rows, preferred_element_type=F32)
        out_ref[:, n : n + step] = (summed - share * resid_ref[:, n : n + step].astype(F32)).astype(out_ref.dtype)


def gradient_kernel(parts_ref, out_ref):
    planes, tokens, width = parts_ref.shape
    missing = parts_ref[0].astype(F32)
    for i in range(1, planes):
        missing = missing + parts_ref[i].astype(F32)
    error = -missing
    spread = jnp.sum(error * error, axis=-1, keepdims=True) * (1.0 / width)
    gradient = (error * lax.rsqrt(spread + 1e-06)).astype(BF16)
    for i in range(planes):
        out_ref[i] = gradient


def spread_kernel(hot_ref, gradient_ref, out_ref):
    groups = out_ref.shape[0]
    count = hot_ref.shape[0]
    width = gradient_ref.shape[1]
    slots = count // groups
    step = 2 * LANES
    for n in range(0, width, step):
        rows = jnp.dot(hot_ref[...], gradient_ref[:, n : n + step], preferred_element_type=F32).astype(BF16)
        for i in range(0, step, LANES):
            at = (n + i) // LANES * slots
            out_ref[:, at : at + slots, :] = rows[:, i : i + LANES].reshape(groups, slots, LANES)


def project_kernel(rows_ref, codes_ref, weight_ref, score_ref, total_ref):
    blocks = rows_ref.shape[0]
    layers, panel, width = weight_ref.shape
    slots = layers * CAP
    halves = panel // LANES
    projections = []
    for l in range(layers):
        rows = jnp.concatenate(
            [
                rows_ref[:, n * slots + l * CAP : n * slots + (l + 1) * CAP, :].reshape(blocks * CAP, LANES)
                for n in range(width // LANES)
            ],
            axis=1,
        )
        projections.append(
            lax.dot_general(rows, weight_ref[l], (((1,), (1,)), ((), ())), preferred_element_type=F32).astype(BF16)
        )
    request = lane_groups(codes_ref[:, halves * slots : halves * slots + 8, :].astype(F32)[:, 1:2, :])
    lane_layer = iota((layers * REQUESTS, LANES), 1) % slots // CAP
    line = iota((layers * REQUESTS, LANES), 0)
    want = (line % REQUESTS + 1).astype(F32)
    here = lane_layer == line // REQUESTS
    member = jnp.concatenate(
        [jnp.where((request[g] == want) & here, 1.0, 0.0) for g in range(blocks * slots // LANES)], axis=1
    ).astype(BF16)
    for h in range(halves):
        values = []
        for l in range(layers):
            at = slice(h * slots + l * CAP, h * slots + (l + 1) * CAP)
            codes = codes_ref[:, at, :].reshape(blocks * CAP, LANES).astype(F32)
            projected = projections[l][:, h * LANES : (h + 1) * LANES].astype(F32)
            value = codes * projected
            score_ref[:, at, :] = value.astype(BF16).reshape(blocks, CAP, LANES)
            values.append(value.reshape(blocks, CAP, LANES))
        value = jnp.concatenate(values, axis=1).reshape(blocks * slots, LANES)
        upper = value.astype(BF16)
        lower = (value - upper.astype(F32)).astype(BF16)
        summed = jnp.dot(member, upper, preferred_element_type=F32) + jnp.dot(
            member, lower, preferred_element_type=F32
        )
        for l in range(layers):
            total_ref[:, l, h * LANES : (h + 1) * LANES] = summed[l * REQUESTS : (l + 1) * REQUESTS]


def place_kernel(slot_ref, scores_ref, out_ref):
    layers, rows = slot_ref.shape
    slots = layers * CAP
    halves = out_ref.shape[3] // LANES
    for l in range(layers):
        column = to_column(slot_ref[l : l + 1, :])
        pick = jnp.where(iota((rows, PANELS * CAP), 1) == column, 1.0, 0.0).astype(BF16)
        scores = jnp.concatenate(
            [
                scores_ref[:, h * slots + l * CAP : h * slots + (l + 1) * CAP, :].reshape(PANELS * CAP, LANES)
                for h in range(halves)
            ],
            axis=1,
        )
        placed = jnp.dot(pick, scores, preferred_element_type=F32).astype(BF16)
        out_ref[l] = placed.reshape(out_ref.shape[1:])


def per_device(feature_codes, block_ids, target_layer, request_ids, target_resid, decoder):
    layers, count, kact, panel = feature_codes.shape
    width = target_resid.shape[1]
    rows = count * kact
    blocks = lax.axis_size(TOK)
    planes = lax.axis_size(COLUMN)
    share = count // planes
    slots = layers * CAP
    code_lines = panel // LANES * slots
    row_lines = width // LANES * slots
    offchip = pl.BlockSpec(memory_space=pltpu.HBM)
    onchip = pl.BlockSpec(memory_space=pltpu.VMEM)
    held = (
        block_ids.transpose(0, 2, 1),
        target_layer.reshape(1, count),
        request_ids.reshape(1, count),
        feature_codes,
        decoder,
    )
    sent, slot, weights = pl.pallas_call(
        pack_kernel,
        out_shape=(
            jax.ShapeDtypeStruct((blocks, code_lines + 8, LANES), BF16),
            jax.ShapeDtypeStruct((layers, rows), jnp.int32),
            jax.ShapeDtypeStruct(decoder.shape, decoder.dtype),
        ),
        in_specs=[offchip] * len(held),
        out_specs=(onchip, onchip, pl.BlockSpec(memory_space=pl.ANY)),
        scratch_shapes=[pltpu.VMEM(a.shape, a.dtype) for a in held[:-1]] + [pltpu.SemaphoreType.DMA((len(held),))],
        compiler_params=pltpu.CompilerParams(vmem_limit_bytes=10 * 1024 * 1024),
        cost_estimate=pl.CostEstimate(flops=300_000_000, bytes_accessed=4_000_000, transcendentals=0),
    )(*[pltpu.with_memory_space_constraint(a, pltpu.HBM) for a in held])
    codes_in = lax.all_to_all(sent, SPREAD, 0, 0, tiled=True)

    built = call(
        build_kernel, jax.ShapeDtypeStruct((blocks, row_lines + 8, LANES), BF16), 1_200_000_000, 8_000_000
    )(codes_in, weights)
    rows_in = lax.all_to_all(built, PLANE, 0, 0, tiled=True)
    partial, hot = call(
        reduce_kernel,
        (jax.ShapeDtypeStruct((count, width), BF16), jax.ShapeDtypeStruct((blocks * slots, count), BF16)),
        600_000_000,
        6_000_000,
    )(rows_in, target_resid)
    parts = lax.all_to_all(partial.reshape(planes, share, width), COLUMN, 0, 0, tiled=True)
    copies = call(gradient_kernel, jax.ShapeDtypeStruct((planes, share, width), BF16), 1_000_000, 1_200_000)(
        parts
    )
    gradient = lax.all_to_all(copies, COLUMN, 0, 0, tiled=True).reshape(count, width)
    spread = call(spread_kernel, jax.ShapeDtypeStruct((blocks, row_lines, LANES), BF16), 600_000_000, 6_000_000)(
        hot, gradient
    )
    grad_in = lax.all_to_all(spread, PLANE, 0, 0, tiled=True)
    scored, totals = call(
        project_kernel,
        (
            jax.ShapeDtypeStruct((blocks, code_lines, LANES), BF16),
            jax.ShapeDtypeStruct((REQUESTS, layers, panel), F32),
        ),
        1_300_000_000,
        8_000_000,
    )(grad_in, codes_in, weights)
    scores_in = lax.all_to_all(scored, SPREAD, 0, 0, tiled=True)
    scores = call(place_kernel, jax.ShapeDtypeStruct(feature_codes.shape, BF16), 140_000_000, 1_000_000)(
        slot, scores_in
    )
    return scores, totals


def solution(mesh):
    fine = Mesh(mesh.devices.reshape(4, 4, 2, 2, 4), EVERY)
    placed = (
        P(LYR, TOK, None, None),
        P(LYR, TOK, None),
        P(TOK),
        P(TOK),
        P(TOK, None),
        P(LYR, TOK, None),
    )
    return jax.shard_map(
        per_device,
        mesh=fine,
        in_specs=placed,
        out_specs=(P(LYR, TOK, None, None), P(None, LYR, TOK)),
        check_vma=False,
    )
```

```python
import jax
import jax.numpy as jnp
from jax import lax
from jax.experimental import pallas as pl
from jax.experimental.pallas import tpu as pltpu
from jax.sharding import Mesh, PartitionSpec as P

PANELS = 32
REQUESTS = 16
CAP = 16
LANES = 128
TOK = ("zh", "x", "c")
SPREAD = ("x", "c", "zh")
LYR = ("zl", "y")
PLANE = ("x", "c", "y")
COLUMN = ("zl", "zh")
EVERY = ("zh", "x", "c", "zl", "y")
BF16 = jnp.bfloat16
F32 = jnp.float32


def call(kernel, out_shape, flops, moved, scratch=(), limit=10):
    return pl.pallas_call(
        kernel,
        out_shape=out_shape,
        scratch_shapes=list(scratch),
        compiler_params=pltpu.CompilerParams(vmem_limit_bytes=limit * 1024 * 1024),
        cost_estimate=pl.CostEstimate(flops=flops, bytes_accessed=moved, transcendentals=0),
    )


def iota(shape, axis):
    return lax.broadcasted_iota(jnp.int32, shape, axis)


def to_column(row):
    n = row.shape[1]
    diag = iota((n, n), 0) == iota((n, n), 1)
    return jnp.sum(jnp.where(diag, jnp.broadcast_to(row, (n, n)), jnp.zeros((n, n), row.dtype)), axis=1, keepdims=True)


def lane_groups(info):
    groups = info.shape[0]
    return jnp.sum(info.reshape(groups // 4, 4, 1, LANES), axis=1)


def pack_kernel(
    ids_hbm, target_hbm, request_hbm, codes_hbm, weight_hbm,
    out_ref, slot_ref, weight_out,
    ids_ref, target_ref, request_ref, codes_ref, sems,
):
    pairs = (
        (ids_hbm, ids_ref), (target_hbm, target_ref), (request_hbm, request_ref), (codes_hbm, codes_ref),
        (weight_hbm, weight_out),
    )
    loads = [pltpu.make_async_copy(source, held, sems.at[i]) for i, (source, held) in enumerate(pairs)]
    for load in loads:
        load.start()
    for load in loads[:-2]:
        load.wait()
    layers, tokens, kact, panel = codes_ref.shape
    rows = kact * tokens
    first_layer = lax.axis_index(LYR) * layers
    slots = layers * CAP
    per = LANES // slots
    halves = panel // LANES
    small = jnp.concatenate([ids_ref[l] for l in range(layers)] + [target_ref[...], request_ref[...]], axis=0)
    small = small.astype(F32).astype(BF16)
    spaced = [
        jnp.dot(
            small,
            jnp.where(iota((tokens, rows), 1) == iota((tokens, rows), 0) * kact + k, 1.0, 0.0).astype(BF16),
            preferred_element_type=F32,
        )
        for k in range(kact)
    ]
    at = layers * kact
    target_row = sum(part[at : at + 1] for part in spaced).astype(jnp.int32)
    request_row = sum(part[at + 1 : at + 2] for part in spaced) + 1.0
    token_row = (iota((1, rows), 1) // kact + 1).astype(F32)
    loads[-2].wait()
    token_info = jnp.zeros((PANELS, LANES), F32)
    request_info = jnp.zeros((PANELS, LANES), F32)
    for l in range(layers):
        panel_id = sum(spaced[k][l * kact + k : l * kact + k + 1] for k in range(kact)).astype(jnp.int32)
        zh, x, c = panel_id // 8, panel_id // 2 % 4, panel_id % 2
        ids_row = (x * 8 + c * 4 + zh).astype(F32)
        ids_col = to_column(ids_row)
        earlier = (ids_col == ids_row) & (iota((rows, rows), 0) < iota((rows, rows), 1))
        rank = jnp.sum(jnp.where(earlier, 1.0, 0.0), axis=0, keepdims=True)
        alive = target_row >= first_layer + l
        slot = jnp.where(alive, (ids_row * CAP + rank).astype(jnp.int32), -1)
        slot_ref[l : l + 1, :] = slot
        pick = jnp.where(iota((PANELS * CAP, rows), 0) == slot, 1.0, 0.0).astype(BF16)
        sent = jnp.dot(pick, codes_ref[l].reshape(rows, panel), preferred_element_type=F32).astype(BF16)
        for h in range(halves):
            half = sent[:, h * LANES : (h + 1) * LANES]
            out_ref[:, h * slots + l * CAP : h * slots + (l + 1) * CAP, :] = half.reshape(PANELS, CAP, LANES)
        named = (iota((PANELS, rows), 0).astype(F32) == ids_row) & alive
        place = jnp.where(iota((rows, LANES), 1) % slots == to_column(rank).astype(jnp.int32) + l * CAP, 1.0, 0.0)
        place = place.astype(BF16)
        token_info += jnp.dot(jnp.where(named, token_row, 0.0).astype(BF16), place, preferred_element_type=F32)
        request_info += jnp.dot(jnp.where(named, request_row, 0.0).astype(BF16), place, preferred_element_type=F32)
    spot = iota((PANELS, LANES), 1) // slots
    token_info = jnp.where(spot == lax.axis_index("y") % per, token_info, 0.0)
    request_info = jnp.where(spot == lax.axis_index(SPREAD) % per, request_info, 0.0)
    line = iota((PANELS, 8, LANES), 1)
    tile = jnp.where(
        line == 0,
        token_info.reshape(PANELS, 1, LANES),
        jnp.where(line == 1, request_info.reshape(PANELS, 1, LANES), 0.0),
    )
    out_ref[:, halves * slots : halves * slots + 8, :] = tile.astype(BF16)
    loads[-1].wait()


def build_kernel(codes_ref, weight_ref, out_ref):
    blocks = codes_ref.shape[0]
    layers, panel, width = weight_ref.shape
    slots = layers * CAP
    halves = panel // LANES
    step = 2 * LANES
    for l in range(layers):
        codes = jnp.concatenate(
            [
                codes_ref[:, h * slots + l * CAP : h * slots + (l + 1) * CAP, :].reshape(blocks * CAP, LANES)
                for h in range(halves)
            ],
            axis=1,
        )
        for n in range(0, width, step):
            built = jnp.dot(codes, weight_ref[l, :, n : n + step], preferred_element_type=F32).astype(BF16)
            for i in range(0, step, LANES):
                at = (n + i) // LANES * slots + l * CAP
                out_ref[:, at : at + CAP, :] = built[:, i : i + LANES].reshape(blocks, CAP, LANES)
    end = width // LANES * slots
    out_ref[:, end : end + 8, :] = codes_ref[:, halves * slots : halves * slots + 8, :]


def reduce_kernel(rows_ref, resid_ref, out_ref, hot_ref):
    groups = rows_ref.shape[0]
    tokens, width = out_ref.shape
    count = hot_ref.shape[0]
    slots = count // groups
    step = 2 * LANES
    end = width // LANES * slots
    token = lane_groups(rows_ref[:, end : end + 8, :].astype(F32)[:, 0:1, :])
    want = (iota((tokens, LANES), 0) + 1).astype(F32)
    hot_t = jnp.concatenate([jnp.where(token[g] == want, 1.0, 0.0) for g in range(count // LANES)], axis=1)
    hot_ref[...] = hot_t.T.astype(BF16)
    hot_t = hot_t.astype(BF16)
    home = (lax.axis_index("zh") == lax.axis_index("y")) & (lax.axis_index("zl") == 0)
    share = jnp.where(home, 1.0, 0.0)
    for n in range(0, width, step):
        rows = jnp.concatenate(
            [
                rows_ref[:, (n + i) // LANES * slots : (n + i) // LANES * slots + slots, :].reshape(count, LANES)
                for i in range(0, step, LANES)
            ],
            axis=1,
        )
        summed = jnp.dot(hot_t, rows, preferred_element_type=F32)
        out_ref[:, n : n + step] = (summed - share * resid_ref[:, n : n + step].astype(F32)).astype(out_ref.dtype)


def gradient_kernel(parts_ref, out_ref):
    planes, tokens, width = parts_ref.shape
    missing = parts_ref[0].astype(F32)
    for i in range(1, planes):
        missing = missing + parts_ref[i].astype(F32)
    error = -missing
    spread = jnp.sum(error * error, axis=-1, keepdims=True) * (1.0 / width)
    gradient = (error * lax.rsqrt(spread + 1e-06)).astype(BF16)
    for i in range(planes):
        out_ref[i] = gradient


def spread_kernel(hot_ref, gradient_ref, out_ref):
    groups = out_ref.shape[0]
    count = hot_ref.shape[0]
    width = gradient_ref.shape[1]
    slots = count // groups
    step = 2 * LANES
    for n in range(0, width, step):
        rows = jnp.dot(hot_ref[...], gradient_ref[:, n : n + step], preferred_element_type=F32).astype(BF16)
        for i in range(0, step, LANES):
            at = (n + i) // LANES * slots
            out_ref[:, at : at + slots, :] = rows[:, i : i + LANES].reshape(groups, slots, LANES)


def project_kernel(rows_ref, codes_ref, weight_ref, score_ref, rest_ref):
    blocks = rows_ref.shape[0]
    layers, panel, width = weight_ref.shape
    slots = layers * CAP
    halves = panel // LANES
    projections = []
    for l in range(layers):
        rows = jnp.concatenate(
            [
                rows_ref[:, n * slots + l * CAP : n * slots + (l + 1) * CAP, :].reshape(blocks * CAP, LANES)
                for n in range(width // LANES)
            ],
            axis=1,
        )
        projections.append(
            lax.dot_general(rows, weight_ref[l], (((1,), (1,)), ((), ())), preferred_element_type=F32).astype(BF16)
        )
    for h in range(halves):
        for l in range(layers):
            at = slice(h * slots + l * CAP, h * slots + (l + 1) * CAP)
            codes = codes_ref[:, at, :].reshape(blocks * CAP, LANES).astype(F32)
            projected = projections[l][:, h * LANES : (h + 1) * LANES].astype(F32)
            value = codes * projected
            upper = value.astype(BF16)
            score_ref[:, at, :] = upper.reshape(blocks, CAP, LANES)
            rest_ref[:, at, :] = (value - upper.astype(F32)).astype(BF16).reshape(blocks, CAP, LANES)


def place_kernel(
    slot_ref, scores_ref, codes_ref, upper_ref, rest_ref, out_hbm, total_hbm, out_ref, total_ref, sems
):
    layers, rows = slot_ref.shape
    blocks = codes_ref.shape[0]
    slots = layers * CAP
    halves = out_ref.shape[3] // LANES
    request = lane_groups(codes_ref[:, halves * slots : halves * slots + 8, :].astype(F32)[:, 1:2, :])
    lane_layer = iota((layers * REQUESTS, LANES), 1) % slots // CAP
    line = iota((layers * REQUESTS, LANES), 0)
    want = (line % REQUESTS + 1).astype(F32)
    here = lane_layer == line // REQUESTS
    member = jnp.concatenate(
        [jnp.where((request[g] == want) & here, 1.0, 0.0) for g in range(blocks * slots // LANES)], axis=1
    ).astype(BF16)
    for h in range(halves):
        lines = slice(h * slots, (h + 1) * slots)
        summed = jnp.dot(
            member, upper_ref[:, lines, :].reshape(blocks * slots, LANES), preferred_element_type=F32
        ) + jnp.dot(member, rest_ref[:, lines, :].reshape(blocks * slots, LANES), preferred_element_type=F32)
        for l in range(layers):
            total_ref[:, l, h * LANES : (h + 1) * LANES] = summed[l * REQUESTS : (l + 1) * REQUESTS]
    copies = [pltpu.make_async_copy(total_ref, total_hbm, sems.at[layers])]
    copies[0].start()
    for l in range(layers):
        column = to_column(slot_ref[l : l + 1, :])
        pick = jnp.where(iota((rows, PANELS * CAP), 1) == column, 1.0, 0.0).astype(BF16)
        scores = jnp.concatenate(
            [
                scores_ref[:, h * slots + l * CAP : h * slots + (l + 1) * CAP, :].reshape(PANELS * CAP, LANES)
                for h in range(halves)
            ],
            axis=1,
        )
        placed = jnp.dot(pick, scores, preferred_element_type=F32).astype(BF16)
        out_ref[l] = placed.reshape(out_ref.shape[1:])
        copies.append(pltpu.make_async_copy(out_ref.at[l], out_hbm.at[l], sems.at[l]))
        copies[-1].start()
    for copy in copies:
        copy.wait()


def per_device(feature_codes, block_ids, target_layer, request_ids, target_resid, decoder):
    layers, count, kact, panel = feature_codes.shape
    width = target_resid.shape[1]
    rows = count * kact
    blocks = lax.axis_size(TOK)
    planes = lax.axis_size(COLUMN)
    share = count // planes
    slots = layers * CAP
    code_lines = panel // LANES * slots
    row_lines = width // LANES * slots
    offchip = pl.BlockSpec(memory_space=pltpu.HBM)
    onchip = pl.BlockSpec(memory_space=pltpu.VMEM)
    held = (
        block_ids.transpose(0, 2, 1),
        target_layer.reshape(1, count),
        request_ids.reshape(1, count),
        feature_codes,
        decoder,
    )
    sent, slot, weights = pl.pallas_call(
        pack_kernel,
        out_shape=(
            jax.ShapeDtypeStruct((blocks, code_lines + 8, LANES), BF16),
            jax.ShapeDtypeStruct((layers, rows), jnp.int32),
            jax.ShapeDtypeStruct(decoder.shape, decoder.dtype),
        ),
        in_specs=[offchip] * len(held),
        out_specs=(onchip, onchip, pl.BlockSpec(memory_space=pl.ANY)),
        scratch_shapes=[pltpu.VMEM(a.shape, a.dtype) for a in held[:-1]] + [pltpu.SemaphoreType.DMA((len(held),))],
        compiler_params=pltpu.CompilerParams(vmem_limit_bytes=10 * 1024 * 1024),
        cost_estimate=pl.CostEstimate(flops=300_000_000, bytes_accessed=4_000_000, transcendentals=0),
    )(*[pltpu.with_memory_space_constraint(a, pltpu.HBM) for a in held])
    codes_in = lax.all_to_all(sent, SPREAD, 0, 0, tiled=True)

    built = call(
        build_kernel, jax.ShapeDtypeStruct((blocks, row_lines + 8, LANES), BF16), 1_200_000_000, 8_000_000
    )(codes_in, weights)
    rows_in = lax.all_to_all(built, PLANE, 0, 0, tiled=True)
    partial, hot = call(
        reduce_kernel,
        (jax.ShapeDtypeStruct((count, width), BF16), jax.ShapeDtypeStruct((blocks * slots, count), BF16)),
        600_000_000,
        6_000_000,
    )(rows_in, target_resid)
    parts = lax.all_to_all(partial.reshape(planes, share, width), COLUMN, 0, 0, tiled=True)
    copies = call(gradient_kernel, jax.ShapeDtypeStruct((planes, share, width), BF16), 1_000_000, 1_200_000)(
        parts
    )
    gradient = lax.all_to_all(copies, COLUMN, 0, 0, tiled=True).reshape(count, width)
    spread = call(spread_kernel, jax.ShapeDtypeStruct((blocks, row_lines, LANES), BF16), 600_000_000, 6_000_000)(
        hot, gradient
    )
    grad_in = lax.all_to_all(spread, PLANE, 0, 0, tiled=True)
    piece = jax.ShapeDtypeStruct((blocks, code_lines, LANES), BF16)
    scored, rest = call(project_kernel, (piece, piece), 1_300_000_000, 8_000_000)(grad_in, codes_in, weights)
    scores_in = lax.all_to_all(scored, SPREAD, 0, 0, tiled=True)
    anywhere = pl.BlockSpec(memory_space=pl.ANY)
    return pl.pallas_call(
        place_kernel,
        out_shape=(
            jax.ShapeDtypeStruct(feature_codes.shape, BF16),
            jax.ShapeDtypeStruct((REQUESTS, layers, panel), F32),
        ),
        out_specs=(anywhere, anywhere),
        scratch_shapes=[
            pltpu.VMEM(feature_codes.shape, BF16),
            pltpu.VMEM((REQUESTS, layers, panel), F32),
            pltpu.SemaphoreType.DMA((layers + 1,)),
        ],
        compiler_params=pltpu.CompilerParams(vmem_limit_bytes=10 * 1024 * 1024),
        cost_estimate=pl.CostEstimate(flops=270_000_000, bytes_accessed=2_000_000, transcendentals=0),
    )(slot, scores_in, codes_in, scored, rest)


def solution(mesh):
    fine = Mesh(mesh.devices.reshape(4, 4, 2, 2, 4), EVERY)
    placed = (
        P(LYR, TOK, None, None),
        P(LYR, TOK, None),
        P(TOK),
        P(TOK),
        P(TOK, None),
        P(LYR, TOK, None),
    )
    return jax.shard_map(
        per_device,
        mesh=fine,
        in_specs=placed,
        out_specs=(P(LYR, TOK, None, None), P(None, LYR, TOK)),
        check_vma=False,
    )
```

```python
import jax
import jax.numpy as jnp
from jax import lax
from jax.experimental import pallas as pl
from jax.experimental.pallas import tpu as pltpu
from jax.sharding import Mesh, PartitionSpec as P

PANELS = 32
REQUESTS = 16
CAP = 16
LANES = 128
TOK = ("zh", "x", "c")
SPREAD = ("x", "c", "zh")
LYR = ("zl", "y")
PLANE = ("x", "c", "y")
COLUMN = ("zl", "zh")
EVERY = ("zh", "x", "c", "zl", "y")
BF16 = jnp.bfloat16
F32 = jnp.float32


def call(kernel, out_shape, flops, moved, scratch=(), limit=10):
    return pl.pallas_call(
        kernel,
        out_shape=out_shape,
        scratch_shapes=list(scratch),
        compiler_params=pltpu.CompilerParams(vmem_limit_bytes=limit * 1024 * 1024),
        cost_estimate=pl.CostEstimate(flops=flops, bytes_accessed=moved, transcendentals=0),
    )


def iota(shape, axis):
    return lax.broadcasted_iota(jnp.int32, shape, axis)


def to_column(row):
    n = row.shape[1]
    diag = iota((n, n), 0) == iota((n, n), 1)
    return jnp.sum(jnp.where(diag, jnp.broadcast_to(row, (n, n)), jnp.zeros((n, n), row.dtype)), axis=1, keepdims=True)


def lane_groups(info):
    groups = info.shape[0]
    return jnp.sum(info.reshape(groups // 4, 4, 1, LANES), axis=1)


def pack_kernel(
    ids_hbm, target_hbm, request_hbm, codes_hbm, weight_hbm,
    out_ref, slot_ref, weight_out,
    ids_ref, target_ref, request_ref, codes_ref, sems,
):
    pairs = (
        (ids_hbm, ids_ref), (target_hbm, target_ref), (request_hbm, request_ref), (codes_hbm, codes_ref),
        (weight_hbm.at[0], weight_out),
    )
    loads = [pltpu.make_async_copy(source, held, sems.at[i]) for i, (source, held) in enumerate(pairs)]
    for load in loads:
        load.start()
    for load in loads[:-2]:
        load.wait()
    layers, tokens, kact, panel = codes_ref.shape
    rows = kact * tokens
    first_layer = lax.axis_index(LYR) * layers
    slots = layers * CAP
    per = LANES // slots
    halves = panel // LANES
    small = jnp.concatenate([ids_ref[l] for l in range(layers)] + [target_ref[...], request_ref[...]], axis=0)
    small = small.astype(F32).astype(BF16)
    spaced = [
        jnp.dot(
            small,
            jnp.where(iota((tokens, rows), 1) == iota((tokens, rows), 0) * kact + k, 1.0, 0.0).astype(BF16),
            preferred_element_type=F32,
        )
        for k in range(kact)
    ]
    at = layers * kact
    target_row = sum(part[at : at + 1] for part in spaced).astype(jnp.int32)
    request_row = sum(part[at + 1 : at + 2] for part in spaced) + 1.0
    token_row = (iota((1, rows), 1) // kact + 1).astype(F32)
    loads[-2].wait()
    token_info = jnp.zeros((PANELS, LANES), F32)
    request_info = jnp.zeros((PANELS, LANES), F32)
    for l in range(layers):
        panel_id = sum(spaced[k][l * kact + k : l * kact + k + 1] for k in range(kact)).astype(jnp.int32)
        zh, x, c = panel_id // 8, panel_id // 2 % 4, panel_id % 2
        ids_row = (x * 8 + c * 4 + zh).astype(F32)
        ids_col = to_column(ids_row)
        earlier = (ids_col == ids_row) & (iota((rows, rows), 0) < iota((rows, rows), 1))
        rank = jnp.sum(jnp.where(earlier, 1.0, 0.0), axis=0, keepdims=True)
        alive = target_row >= first_layer + l
        slot = jnp.where(alive, (ids_row * CAP + rank).astype(jnp.int32), -1)
        slot_ref[l : l + 1, :] = slot
        pick = jnp.where(iota((PANELS * CAP, rows), 0) == slot, 1.0, 0.0).astype(BF16)
        sent = jnp.dot(pick, codes_ref[l].reshape(rows, panel), preferred_element_type=F32).astype(BF16)
        for h in range(halves):
            half = sent[:, h * LANES : (h + 1) * LANES]
            out_ref[:, h * slots + l * CAP : h * slots + (l + 1) * CAP, :] = half.reshape(PANELS, CAP, LANES)
        named = (iota((PANELS, rows), 0).astype(F32) == ids_row) & alive
        place = jnp.where(iota((rows, LANES), 1) % slots == to_column(rank).astype(jnp.int32) + l * CAP, 1.0, 0.0)
        place = place.astype(BF16)
        token_info += jnp.dot(jnp.where(named, token_row, 0.0).astype(BF16), place, preferred_element_type=F32)
        request_info += jnp.dot(jnp.where(named, request_row, 0.0).astype(BF16), place, preferred_element_type=F32)
    spot = iota((PANELS, LANES), 1) // slots
    token_info = jnp.where(spot == lax.axis_index("y") % per, token_info, 0.0)
    request_info = jnp.where(spot == lax.axis_index(SPREAD) % per, request_info, 0.0)
    line = iota((PANELS, 8, LANES), 1)
    tile = jnp.where(
        line == 0,
        token_info.reshape(PANELS, 1, LANES),
        jnp.where(line == 1, request_info.reshape(PANELS, 1, LANES), 0.0),
    )
    out_ref[:, halves * slots : halves * slots + 8, :] = tile.astype(BF16)
    loads[-1].wait()


def build_kernel(codes_ref, first_ref, weight_hbm, out_ref, rest_ref, rest_sem):
    load = pltpu.make_async_copy(weight_hbm.at[1:], rest_ref, rest_sem)
    load.start()
    blocks = codes_ref.shape[0]
    layers, panel, width = weight_hbm.shape
    slots = layers * CAP
    halves = panel // LANES
    step = 2 * LANES
    for l in range(layers):
        codes = jnp.concatenate(
            [
                codes_ref[:, h * slots + l * CAP : h * slots + (l + 1) * CAP, :].reshape(blocks * CAP, LANES)
                for h in range(halves)
            ],
            axis=1,
        )
        if l == 1:
            load.wait()
        for n in range(0, width, step):
            weight = first_ref[:, n : n + step] if l == 0 else rest_ref[l - 1, :, n : n + step]
            built = jnp.dot(codes, weight, preferred_element_type=F32).astype(BF16)
            for i in range(0, step, LANES):
                at = (n + i) // LANES * slots + l * CAP
                out_ref[:, at : at + CAP, :] = built[:, i : i + LANES].reshape(blocks, CAP, LANES)
    end = width // LANES * slots
    out_ref[:, end : end + 8, :] = codes_ref[:, halves * slots : halves * slots + 8, :]


def reduce_kernel(rows_ref, resid_ref, out_ref, hot_ref):
    groups = rows_ref.shape[0]
    tokens, width = out_ref.shape
    count = hot_ref.shape[0]
    slots = count // groups
    step = 2 * LANES
    end = width // LANES * slots
    token = lane_groups(rows_ref[:, end : end + 8, :].astype(F32)[:, 0:1, :])
    want = (iota((tokens, LANES), 0) + 1).astype(F32)
    hot_t = jnp.concatenate([jnp.where(token[g] == want, 1.0, 0.0) for g in range(count // LANES)], axis=1)
    hot_ref[...] = hot_t.T.astype(BF16)
    hot_t = hot_t.astype(BF16)
    home = (lax.axis_index("zh") == lax.axis_index("y")) & (lax.axis_index("zl") == 0)
    share = jnp.where(home, 1.0, 0.0)
    for n in range(0, width, step):
        rows = jnp.concatenate(
            [
                rows_ref[:, (n + i) // LANES * slots : (n + i) // LANES * slots + slots, :].reshape(count, LANES)
                for i in range(0, step, LANES)
            ],
            axis=1,
        )
        summed = jnp.dot(hot_t, rows, preferred_element_type=F32)
        out_ref[:, n : n + step] = (summed - share * resid_ref[:, n : n + step].astype(F32)).astype(out_ref.dtype)


def gradient_kernel(parts_ref, out_ref):
    planes, tokens, width = parts_ref.shape
    missing = parts_ref[0].astype(F32)
    for i in range(1, planes):
        missing = missing + parts_ref[i].astype(F32)
    error = -missing
    spread = jnp.sum(error * error, axis=-1, keepdims=True) * (1.0 / width)
    gradient = (error * lax.rsqrt(spread + 1e-06)).astype(BF16)
    for i in range(planes):
        out_ref[i] = gradient


def spread_kernel(hot_ref, gradient_ref, out_ref):
    groups = out_ref.shape[0]
    count = hot_ref.shape[0]
    width = gradient_ref.shape[1]
    slots = count // groups
    step = 2 * LANES
    for n in range(0, width, step):
        rows = jnp.dot(hot_ref[...], gradient_ref[:, n : n + step], preferred_element_type=F32).astype(BF16)
        for i in range(0, step, LANES):
            at = (n + i) // LANES * slots
            out_ref[:, at : at + slots, :] = rows[:, i : i + LANES].reshape(groups, slots, LANES)


def project_kernel(rows_ref, codes_ref, first_ref, weights_ref, score_ref, rest_ref):
    blocks = rows_ref.shape[0]
    panel, width = first_ref.shape
    layers = weights_ref.shape[0] + 1
    slots = layers * CAP
    halves = panel // LANES
    projections = []
    for l in range(layers):
        rows = jnp.concatenate(
            [
                rows_ref[:, n * slots + l * CAP : n * slots + (l + 1) * CAP, :].reshape(blocks * CAP, LANES)
                for n in range(width // LANES)
            ],
            axis=1,
        )
        projections.append(
            lax.dot_general(rows, first_ref[...] if l == 0 else weights_ref[l - 1], (((1,), (1,)), ((), ())), preferred_element_type=F32).astype(BF16)
        )
    for h in range(halves):
        for l in range(layers):
            at = slice(h * slots + l * CAP, h * slots + (l + 1) * CAP)
            codes = codes_ref[:, at, :].reshape(blocks * CAP, LANES).astype(F32)
            projected = projections[l][:, h * LANES : (h + 1) * LANES].astype(F32)
            value = codes * projected
            upper = value.astype(BF16)
            score_ref[:, at, :] = upper.reshape(blocks, CAP, LANES)
            rest_ref[:, at, :] = (value - upper.astype(F32)).astype(BF16).reshape(blocks, CAP, LANES)


def place_kernel(
    slot_ref, scores_ref, codes_ref, upper_ref, rest_ref, out_hbm, total_hbm, out_ref, total_ref, sems
):
    layers, rows = slot_ref.shape
    blocks = codes_ref.shape[0]
    slots = layers * CAP
    halves = out_ref.shape[3] // LANES
    request = lane_groups(codes_ref[:, halves * slots : halves * slots + 8, :].astype(F32)[:, 1:2, :])
    lane_layer = iota((layers * REQUESTS, LANES), 1) % slots // CAP
    line = iota((layers * REQUESTS, LANES), 0)
    want = (line % REQUESTS + 1).astype(F32)
    here = lane_layer == line // REQUESTS
    member = jnp.concatenate(
        [jnp.where((request[g] == want) & here, 1.0, 0.0) for g in range(blocks * slots // LANES)], axis=1
    ).astype(BF16)
    for h in range(halves):
        lines = slice(h * slots, (h + 1) * slots)
        summed = jnp.dot(
            member, upper_ref[:, lines, :].reshape(blocks * slots, LANES), preferred_element_type=F32
        ) + jnp.dot(member, rest_ref[:, lines, :].reshape(blocks * slots, LANES), preferred_element_type=F32)
        for l in range(layers):
            total_ref[:, l, h * LANES : (h + 1) * LANES] = summed[l * REQUESTS : (l + 1) * REQUESTS]
    copies = [pltpu.make_async_copy(total_ref, total_hbm, sems.at[layers])]
    copies[0].start()
    for l in range(layers):
        column = to_column(slot_ref[l : l + 1, :])
        pick = jnp.where(iota((rows, PANELS * CAP), 1) == column, 1.0, 0.0).astype(BF16)
        scores = jnp.concatenate(
            [
                scores_ref[:, h * slots + l * CAP : h * slots + (l + 1) * CAP, :].reshape(PANELS * CAP, LANES)
                for h in range(halves)
            ],
            axis=1,
        )
        placed = jnp.dot(pick, scores, preferred_element_type=F32).astype(BF16)
        out_ref[l] = placed.reshape(out_ref.shape[1:])
        copies.append(pltpu.make_async_copy(out_ref.at[l], out_hbm.at[l], sems.at[l]))
        copies[-1].start()
    for copy in copies:
        copy.wait()


def per_device(feature_codes, block_ids, target_layer, request_ids, target_resid, decoder):
    layers, count, kact, panel = feature_codes.shape
    width = target_resid.shape[1]
    rows = count * kact
    blocks = lax.axis_size(TOK)
    planes = lax.axis_size(COLUMN)
    share = count // planes
    slots = layers * CAP
    code_lines = panel // LANES * slots
    row_lines = width // LANES * slots
    offchip = pl.BlockSpec(memory_space=pltpu.HBM)
    onchip = pl.BlockSpec(memory_space=pltpu.VMEM)
    held = (
        block_ids.transpose(0, 2, 1),
        target_layer.reshape(1, count),
        request_ids.reshape(1, count),
        feature_codes,
        decoder,
    )
    sent, slot, first = pl.pallas_call(
        pack_kernel,
        out_shape=(
            jax.ShapeDtypeStruct((blocks, code_lines + 8, LANES), BF16),
            jax.ShapeDtypeStruct((layers, rows), jnp.int32),
            jax.ShapeDtypeStruct(decoder.shape[1:], decoder.dtype),
        ),
        in_specs=[offchip] * len(held),
        out_specs=(onchip, onchip, pl.BlockSpec(memory_space=pl.ANY)),
        scratch_shapes=[pltpu.VMEM(a.shape, a.dtype) for a in held[:-1]] + [pltpu.SemaphoreType.DMA((len(held),))],
        compiler_params=pltpu.CompilerParams(vmem_limit_bytes=10 * 1024 * 1024),
        cost_estimate=pl.CostEstimate(flops=300_000_000, bytes_accessed=4_000_000, transcendentals=0),
    )(*[pltpu.with_memory_space_constraint(a, pltpu.HBM) for a in held])
    codes_in = lax.all_to_all(sent, SPREAD, 0, 0, tiled=True)

    built, rest_weights = pl.pallas_call(
        build_kernel,
        out_shape=(
            jax.ShapeDtypeStruct((blocks, row_lines + 8, LANES), BF16),
            jax.ShapeDtypeStruct((layers - 1,) + decoder.shape[1:], decoder.dtype),
        ),
        in_specs=[onchip, onchip, offchip],
        out_specs=(onchip, pl.BlockSpec(memory_space=pltpu.VMEM)),
        scratch_shapes=[pltpu.SemaphoreType.DMA],
        compiler_params=pltpu.CompilerParams(vmem_limit_bytes=10 * 1024 * 1024),
        cost_estimate=pl.CostEstimate(flops=1_200_000_000, bytes_accessed=8_000_000, transcendentals=0),
    )(codes_in, first, pltpu.with_memory_space_constraint(decoder, pltpu.HBM))
    rows_in = lax.all_to_all(built, PLANE, 0, 0, tiled=True)
    partial, hot = call(
        reduce_kernel,
        (jax.ShapeDtypeStruct((count, width), BF16), jax.ShapeDtypeStruct((blocks * slots, count), BF16)),
        600_000_000,
        6_000_000,
    )(rows_in, target_resid)
    parts = lax.all_to_all(partial.reshape(planes, share, width), COLUMN, 0, 0, tiled=True)
    copies = call(gradient_kernel, jax.ShapeDtypeStruct((planes, share, width), BF16), 1_000_000, 1_200_000)(
        parts
    )
    gradient = lax.all_to_all(copies, COLUMN, 0, 0, tiled=True).reshape(count, width)
    spread = call(spread_kernel, jax.ShapeDtypeStruct((blocks, row_lines, LANES), BF16), 600_000_000, 6_000_000)(
        hot, gradient
    )
    grad_in = lax.all_to_all(spread, PLANE, 0, 0, tiled=True)
    piece = jax.ShapeDtypeStruct((blocks, code_lines, LANES), BF16)
    scored, rest = call(project_kernel, (piece, piece), 1_300_000_000, 8_000_000)(
        grad_in, codes_in, first, rest_weights
    )
    scores_in = lax.all_to_all(scored, SPREAD, 0, 0, tiled=True)
    anywhere = pl.BlockSpec(memory_space=pl.ANY)
    return pl.pallas_call(
        place_kernel,
        out_shape=(
            jax.ShapeDtypeStruct(feature_codes.shape, BF16),
            jax.ShapeDtypeStruct((REQUESTS, layers, panel), F32),
        ),
        out_specs=(anywhere, anywhere),
        scratch_shapes=[
            pltpu.VMEM(feature_codes.shape, BF16),
            pltpu.VMEM((REQUESTS, layers, panel), F32),
            pltpu.SemaphoreType.DMA((layers + 1,)),
        ],
        compiler_params=pltpu.CompilerParams(vmem_limit_bytes=10 * 1024 * 1024),
        cost_estimate=pl.CostEstimate(flops=270_000_000, bytes_accessed=2_000_000, transcendentals=0),
    )(slot, scores_in, codes_in, scored, rest)


def solution(mesh):
    fine = Mesh(mesh.devices.reshape(4, 4, 2, 2, 4), EVERY)
    placed = (
        P(LYR, TOK, None, None),
        P(LYR, TOK, None),
        P(TOK),
        P(TOK),
        P(TOK, None),
        P(LYR, TOK, None),
    )
    return jax.shard_map(
        per_device,
        mesh=fine,
        in_specs=placed,
        out_specs=(P(LYR, TOK, None, None), P(None, LYR, TOK)),
        check_vma=False,
    )
```
